256 devices in a mesh: row: 8 (over y, core), col: 32 (over z, x).
Axes of the slice: x: 4, y: 4, z: 8, core: 2. Of those that a mesh axis runs over, the one named last changes fastest.
Arguments:
- field: float32 [32, 256, 16384], P(None, 'row', 'col'), may hold values from -4 to 4
- right_side: float32 [32, 256, 16384], P(None, 'row', 'col'), may hold values from -6 to 6
- kappa: float32 [256, 16384], P('row', 'col'), may hold values from 0.1 to 3
- fronts: bfloat16 [8, 4096, 16384], P(None, 'row', 'col'), may hold values from -2 to 2
Outputs:
- residual: float32 [32, 256, 16384], P(None, 'row', 'col')
- separator_solution: float32 [256, 16384], P('row', 'col')
The draws below stay inside these ranges and needn't reach their ends.
All inputs are finite; a program needn't handle non-finite values.
Results may differ from the reference program's by a relative error of at most 0.022.
Values sent between devices are 32-bit elements; how exact they have to be, the bound alone decides.
A program may use at most 64 MiB of HBM per device.

```python
import math
import jax
import jax.numpy as jnp
from jax import lax

K = 32
SEP = 512
CR = 32
COL_BITS = 5
LEVELS = 8
NR = 256
NC = 16384
FR = 4096
N_ROW = 8
N_COL = 32


def draw_fronts(key, part):
    shape = (LEVELS, FR, NC)
    noise = jnp.clip(jax.random.normal(key, shape, jnp.float32), -4.0, 4.0)
    noise = noise * (0.4 / math.sqrt(SEP))
    row_idx = jnp.arange(FR, dtype=jnp.int32)[None, :, None]
    col_idx = jnp.arange(NC, dtype=jnp.int32)[None, None, :]
    diagonal = row_idx % SEP == col_idx % SEP
    return (noise + jnp.where(diagonal, 0.7, 0.0)).astype(jnp.bfloat16)


def block_levels(stream_key, extent, pieces, least, top_value):
    loudness = 1.0
    for axis_at, shards_of in pieces:
        heights = jax.random.uniform(jax.random.fold_in(jax.random.fold_in(stream_key, 6), axis_at), (shards_of,), jnp.float32, least / len(pieces), top_value / len(pieces))
        loudness = loudness * jnp.repeat(jnp.exp(heights), extent[axis_at] // shards_of).reshape((-1,) + (1,) * (len(extent) - 1 - axis_at))
    return loudness


def bell_draw(key, shape, deviation, bound, split=(), kind=jnp.bfloat16):
    loudness = block_levels(key, shape, split, -0.22, 0.18) if split else 1.0
    values = jax.random.normal(key, shape, jnp.float32) * deviation * loudness
    return jnp.minimum(jnp.maximum(values, -bound), bound).astype(kind)


def setup_inputs(seed: int = 0) -> dict:
    key_of = jax.random.split(jax.random.key(seed), 5)
    return {
        "field": bell_draw(key_of[0], (K, NR, NC), 0.5, 4.0, ((1, 8), (2, 32)), jnp.float32),
        "right_side": bell_draw(key_of[1], (K, NR, NC), 1.0, 6.0, ((1, 8), (2, 32)), jnp.float32),
        "kappa": jnp.clip(jnp.exp(math.log(3.0) - 3.4011974 * jax.random.uniform(key_of[2], (NR, NC), jnp.float32) ** block_levels(key_of[2], (NR, NC), ((0, 8), (1, 32)), -0.2, 0.2)), 0.1, 3.0),
        "fronts": draw_fronts(jax.random.fold_in(key_of[4], 71), 0),
    }


def rounded(value):
    return lax.optimization_barrier(value.astype(jnp.bfloat16)).astype(jnp.float32)


def level_setup(level):
    rows_idx = jnp.arange(N_ROW, dtype=jnp.int32)
    cols_idx = jnp.arange(N_COL, dtype=jnp.int32)
    if level < COL_BITS:
        lower = jnp.bitwise_and(jnp.right_shift(cols_idx, level), 1) == 0
        lower = jnp.broadcast_to(lower[None, :], (N_ROW, N_COL))
        partner = jnp.bitwise_xor(cols_idx, 1 << level).astype(jnp.int32)
        axis_pick = 1
    else:
        shift_by = level - COL_BITS
        lower = jnp.bitwise_and(jnp.right_shift(rows_idx, shift_by), 1) == 0
        lower = jnp.broadcast_to(lower[:, None], (N_ROW, N_COL))
        partner = jnp.bitwise_xor(rows_idx, 1 << shift_by).astype(jnp.int32)
        axis_pick = 0
    return lower[:, :, None, None], partner, axis_pick


def reference(field, right_side, kappa, fronts):
    padded = jnp.pad(field, ((0, 0), (1, 1), (1, 1)))
    near = padded[:, 2:, 1:-1] + padded[:, :-2, 1:-1] + padded[:, 1:-1, 2:] + padded[:, 1:-1, :-2]
    residual = right_side - ((4.0 + kappa) * field - near)
    edge = residual[:, CR - 1::CR, :]
    state = edge.reshape(K, N_ROW, N_COL, SEP).transpose(1, 2, 0, 3)
    for level in range(LEVELS):
        lower, partner, axis_pick = level_setup(level)
        front = fronts[level].reshape(N_ROW, SEP, N_COL, SEP).astype(jnp.float32)
        first = jnp.einsum('rcka,racb->rckb', rounded(state), front)
        got = jnp.take(first, partner, axis=axis_pick)
        state = jnp.where(lower, first + got, got - first)
    for level in range(LEVELS - 1, -1, -1):
        lower, partner, axis_pick = level_setup(level)
        front = fronts[level].reshape(N_ROW, SEP, N_COL, SEP).astype(jnp.float32)
        got = jnp.take(state, partner, axis=axis_pick)
        combined = jnp.where(lower, state - got, state + got)
        state = jnp.einsum('rcka,rbca->rckb', rounded(combined), front)
    separator_solution = state.transpose(0, 2, 1, 3).reshape(N_ROW * K, N_COL * SEP)
    return residual, separator_solution
```

```python
import functools

import jax
import jax.numpy as jnp
from jax import lax
from jax.experimental import pallas as pl
from jax.experimental.pallas import tpu as pltpu
from jax.sharding import PartitionSpec as P

MESH = pl.DeviceIdType.MESH
LANES = 128
CHUNKS = 4


def kernel(
    sizes,
    field, right_side, kappa, fronts,
    residual, separator,
    cells, sources, shift, result, weights,
    first_row, last_row, below, above, edge_left, edge_right,
    rim_first, rim_last, rim_left, rim_right,
    sent, got,
    load_sem, front_sem, store_sem, halo_send, halo_recv, send_sem, recv_sem,
):
    k_count, depth, width, levels, col_bits, n_row, n_col = sizes
    row = lax.axis_index("row")
    col = lax.axis_index("col")
    rows_per = k_count // CHUNKS

    def partner(level):
        if level < col_bits:
            return {"col": jnp.bitwise_xor(col, 1 << level)}
        return {"row": jnp.bitwise_xor(row, 1 << (level - col_bits))}

    def sign(level):
        place = col if level < col_bits else row
        bit = level if level < col_bits else level - col_bits
        upper = jnp.bitwise_and(jnp.right_shift(place, bit), 1)
        return 1.0 - 2.0 * upper.astype(jnp.float32)

    up = {"row": lax.rem(row + n_row - 1, n_row)}
    down = {"row": lax.rem(row + 1, n_row)}
    left = {"col": lax.rem(col + n_col - 1, n_col)}
    right = {"col": lax.rem(col + 1, n_col)}

    barrier = pltpu.get_barrier_semaphore()
    friends = [partner(level) for level in range(levels)] + [up, down, left, right]
    for friend in friends:
        pl.semaphore_signal(barrier, inc=1, device_id=friend, device_id_type=MESH)

    loads = [
        pltpu.make_async_copy(field, cells, load_sem.at[0]),
        pltpu.make_async_copy(right_side, sources, load_sem.at[1]),
        pltpu.make_async_copy(kappa, shift, load_sem.at[2]),
    ]
    for load in loads:
        load.start()
    front_loads = [
        pltpu.make_async_copy(fronts.at[level], weights.at[level], front_sem.at[level])
        for level in range(levels)
    ]
    for load in front_loads:
        load.start()

    def halo(slot, source, target, device):
        return pltpu.make_async_remote_copy(
            src_ref=source,
            dst_ref=target,
            send_sem=halo_send.at[slot],
            recv_sem=halo_recv.at[slot],
            device_id=device,
            device_id_type=MESH,
        )

    halos = [
        halo(0, first_row, below, up),
        halo(1, last_row.at[:, pl.ds(width - LANES, LANES)], edge_left, right),
        halo(2, last_row.at[:, pl.ds(0, LANES)], edge_right, left),
        halo(3, last_row, above, down),
        halo(4, rim_last, rim_left, right),
        halo(5, rim_first, rim_right, left),
    ]

    loads[0].wait()
    first_row[...] = cells[:, 0, :]
    last_row[...] = cells[:, depth - 1, :]
    pl.semaphore_wait(barrier, len(friends))
    for slot in range(4):
        halos[slot].start()

    rim_lane = lax.broadcasted_iota(jnp.int32, (depth, LANES), 1)
    firsts = jnp.zeros((depth, LANES), jnp.float32)
    lasts = jnp.zeros((depth, LANES), jnp.float32)
    for k in range(k_count):
        head = cells[k, :, pl.ds(0, LANES)]
        tail = cells[k, :, pl.ds(width - LANES, LANES)]
        firsts = jnp.where(rim_lane == k, pltpu.roll(head, k, 1) if k else head, firsts)
        lasts = jnp.where(rim_lane == k, pltpu.roll(tail, k + 1, 1), lasts)
    rim_first[...] = firsts
    rim_last[...] = lasts
    halos[4].start()
    halos[5].start()

    has_above = (row > 0).astype(jnp.float32)
    has_below = (row < n_row - 1).astype(jnp.float32)
    has_left = (col > 0).astype(jnp.float32)
    has_right = (col < n_col - 1).astype(jnp.float32)

    def beside(block, right_edge, left_edge):
        lane = lax.broadcasted_iota(jnp.int32, block.shape, 1)
        from_right = jnp.where(lane == width - 1, right_edge, pltpu.roll(block, width - 1, 1))
        from_left = jnp.where(lane == 0, left_edge, pltpu.roll(block, 1, 1))
        return from_right, from_left

    def level_step(stage, chunk, state, level, transposed):
        dims = (((1,), (1,)), ((), ())) if transposed else (((1,), (0,)), ((), ()))
        return lax.dot_general(
            state.astype(jnp.bfloat16),
            weights[level],
            dims,
            preferred_element_type=jnp.float32,
        )

    exchanges = 2 * levels - 1

    def exchange(index, chunk):
        level = index if index < levels else 2 * levels - 2 - index
        part = pl.ds(chunk * rows_per, rows_per)
        return pltpu.make_async_remote_copy(
            src_ref=sent.at[index, part],
            dst_ref=got.at[index, part],
            send_sem=send_sem.at[index, chunk],
            recv_sem=recv_sem.at[index, chunk],
            device_id=partner(level),
            device_id_type=MESH,
        )

    def piece(k):
        block = cells[k]
        line = lax.broadcasted_iota(jnp.int32, block.shape, 0)
        under = jnp.where(
            line == depth - 1, below[pl.ds(k, 1), :] * has_below, pltpu.roll(block, depth - 1, 0)
        )
        over = jnp.where(line == 0, above[pl.ds(k, 1), :] * has_above, pltpu.roll(block, 1, 0))
        from_right, from_left = beside(
            block,
            rim_right[:, pl.ds(k, 1)] * has_right,
            rim_left[:, pl.ds(k, 1)] * has_left,
        )
        near = under + over + from_right + from_left
        result[k] = sources[k] - ((4.0 + shift[...]) * block - near)

    for load in loads[1:]:
        load.wait()
    shift_last = shift[pl.ds(depth - 1, 1), :]
    for slot in range(3):
        halos[slot].wait_recv()

    for chunk in range(CHUNKS):
        part = pl.ds(chunk * rows_per, rows_per)
        block = last_row[part, :]
        over = cells[part, depth - 2, :]
        source = sources[part, depth - 1, :]
        under = below[part, :] * has_below
        from_right, from_left = beside(
            block,
            edge_right[part, pl.ds(0, 1)] * has_right,
            edge_left[part, pl.ds(LANES - 1, 1)] * has_left,
        )
        near = under + over + from_right + from_left
        state = source - ((4.0 + shift_last) * block - near)
        if chunk == 0:
            front_loads[0].wait()
        sent[0, part] = level_step(0, chunk, state, 0, False)
        exchange(0, chunk).start()

    for slot in range(3, 6):
        halos[slot].wait_recv()

    pieces = list(range(k_count))
    slots = max(1, (exchanges - 1) * CHUNKS)
    done = 0
    gap = 0
    for stage in range(1, exchanges + 1):
        index = stage - 1
        forward = stage < levels
        level = stage if forward else 2 * levels - 1 - stage
        if forward:
            front_loads[level].wait()
        for chunk in range(CHUNKS):
            part = pl.ds(chunk * rows_per, rows_per)
            exchange(index, chunk).wait_recv()
            other = got[index, part]
            if forward:
                state = other + sign(level - 1) * sent[index, part]
            elif stage == levels:
                state = 2.0 * other
            else:
                state = sent[index, part] - sign(level) * other
            product = level_step(stage, chunk, state, level, not forward)
            if stage < exchanges:
                sent[stage, part] = product
                exchange(stage, chunk).start()
                gap += 1
                while pieces and done * slots < gap * k_count:
                    piece(pieces.pop(0))
                    done += 1
                    if done == k_count:
                        store = pltpu.make_async_copy(result, residual, store_sem)
                        store.start()
            else:
                separator[part, :] = product

    store.wait()
    for slot in range(6):
        halos[slot].wait_send()
    for index in range(exchanges):
        for chunk in range(CHUNKS):
            exchange(index, chunk).wait_send()


def body(field, right_side, kappa, fronts):
    k_count, depth, width = field.shape
    n_row = lax.axis_size("row")
    n_col = lax.axis_size("col")
    col_bits = n_col.bit_length() - 1
    levels = col_bits + n_row.bit_length() - 1
    exchanges = 2 * levels - 1
    f32 = jnp.float32
    whole = pl.BlockSpec(memory_space=pl.ANY)
    dma = pltpu.SemaphoreType.DMA
    residual, separator = pl.pallas_call(
        functools.partial(kernel, (k_count, depth, width, levels, col_bits, n_row, n_col)),
        out_shape=(
            jax.ShapeDtypeStruct((k_count, depth, width), f32),
            jax.ShapeDtypeStruct((k_count, width), f32),
        ),
        in_specs=[pl.BlockSpec(memory_space=pltpu.HBM)] * 4,
        out_specs=(whole, pl.BlockSpec(memory_space=pltpu.VMEM)),
        scratch_shapes=[
            pltpu.VMEM((k_count, depth, width), f32),
            pltpu.VMEM((k_count, depth, width), f32),
            pltpu.VMEM((depth, width), f32),
            pltpu.VMEM((k_count, depth, width), f32),
            pltpu.VMEM((levels, width, width), jnp.bfloat16),
            pltpu.VMEM((k_count, width), f32),
            pltpu.VMEM((k_count, width), f32),
            pltpu.VMEM((k_count, width), f32),
            pltpu.VMEM((k_count, width), f32),
            pltpu.VMEM((k_count, LANES), f32),
            pltpu.VMEM((k_count, LANES), f32),
            pltpu.VMEM((depth, LANES), f32),
            pltpu.VMEM((depth, LANES), f32),
            pltpu.VMEM((depth, LANES), f32),
            pltpu.VMEM((depth, LANES), f32),
            pltpu.VMEM((exchanges, k_count, width), f32),
            pltpu.VMEM((exchanges, k_count, width), f32),
            dma((3,)),
            dma((levels,)),
            dma,
            dma((6,)),
            dma((6,)),
            dma((exchanges, CHUNKS)),
            dma((exchanges, CHUNKS)),
        ],
        compiler_params=pltpu.CompilerParams(
            collective_id=0, has_side_effects=True, vmem_limit_bytes=67043328
        ),
    )(
        field,
        right_side,
        kappa,
        fronts,
    )
    return (residual, separator)


def solution(mesh):
    placed = (P(None, "row", "col"), P(None, "row", "col"), P("row", "col"), P(None, "row", "col"))
    return jax.shard_map(
        body,
        mesh=mesh,
        in_specs=placed,
        out_specs=(P(None, "row", "col"), P("row", "col")),
        check_vma=False,
    )
```

```python
import functools

import jax
import jax.numpy as jnp
from jax import lax
from jax.experimental import pallas as pl
from jax.experimental.pallas import tpu as pltpu
from jax.sharding import PartitionSpec as P

MESH = pl.DeviceIdType.MESH
LANES = 128
CHUNKS = 4
PIECE = 32


def back_groups(levels, col_bits):
    groups = []
    level = levels - 1
    while level >= 0:
        row_pair = level == levels - 1 and level - 1 >= col_bits
        col_pair = level % 2 == 1 and level < col_bits and level <= 3
        if row_pair or col_pair:
            groups.append((level, level - 1))
            level -= 2
        else:
            groups.append((level,))
            level -= 1
    return groups


def group_targets(group, top):
    if len(group) == 1:
        return [group]
    a, b = group
    return [(a,), (a, b)] if top else [(a,), (b,), (a, b)]


def phase_plan(levels, col_bits):
    groups = back_groups(levels, col_bits)
    targets = [[(level,)] for level in range(levels - 1)]
    targets.append(group_targets(groups[0], True))
    for group in groups[1:]:
        targets.append(group_targets(group, False))
    return groups, targets


def kernel(
    sizes,
    field, right_side, kappa, fronts,
    residual, separator,
    cells, sources, shift, weights, extra, bulk_out, bulk_in,
    first_row, last_row, below, above, edge_left, edge_right,
    rim_first, rim_last, rim_left, rim_right,
    sent, got,
    load_sem, front_sem, halo_send, halo_recv, send_sem, recv_sem, bulk_send, bulk_recv,
    col_ready, row_ready,
):
    k_count, depth, width, levels, col_bits, n_row, n_col = sizes
    row = lax.axis_index("row")
    col = lax.axis_index("col")
    rows_per = k_count // CHUNKS
    groups, targets = phase_plan(levels, col_bits)
    phases = len(targets)
    pairs = [group for group in groups if len(group) == 2]
    row_bits = levels - col_bits
    piece_count = width // PIECE

    def flip(toggled):
        if toggled[0] < col_bits:
            return {"col": jnp.bitwise_xor(col, sum(1 << level for level in toggled))}
        return {"row": jnp.bitwise_xor(row, sum(1 << (level - col_bits) for level in toggled))}

    def sign(level):
        place = col if level < col_bits else row
        bit = level if level < col_bits else level - col_bits
        upper = jnp.bitwise_and(jnp.right_shift(place, bit), 1)
        return 1.0 - 2.0 * upper.astype(jnp.float32)

    def row_at(step):
        return {"row": lax.rem(row + (n_row + step) % n_row, n_row)}

    def col_at(step):
        return {"col": lax.rem(col + (n_col + step) % n_col, n_col)}

    up, down, left, right = row_at(-1), row_at(1), col_at(-1), col_at(1)

    barrier = pltpu.get_barrier_semaphore()
    friends = [up, down, left, right] + [flip((b,)) for a, b in pairs]
    for friend in friends:
        pl.semaphore_signal(barrier, inc=1, device_id=friend, device_id_type=MESH)

    def tell(step):
        for ready, at, bits in ((col_ready, col_at, col_bits), (row_ready, row_at, row_bits)):
            if step < bits:
                for way, sense in ((0, 1), (1, -1)):
                    pl.semaphore_signal(
                        ready.at[step, way],
                        inc=1,
                        device_id=at(sense * (1 << (step - 1))),
                        device_id_type=MESH,
                    )

    def hear(step):
        for ready, bits in ((col_ready, col_bits), (row_ready, row_bits)):
            if step < bits:
                for way in range(2):
                    pl.semaphore_wait(ready.at[step, way], 1)

    loads = [
        pltpu.make_async_copy(field, cells, load_sem.at[0]),
        pltpu.make_async_copy(right_side, sources, load_sem.at[1]),
        pltpu.make_async_copy(kappa, shift, load_sem.at[2]),
    ]
    front_loads = [
        pltpu.make_async_copy(fronts.at[level], weights.at[level], front_sem.at[level])
        for level in range(levels)
    ]
    loads[0].start()
    front_loads[0].start()
    loads[1].start()
    loads[2].start()
    order = [pair[0] for pair in pairs]
    order += [level for level in range(1, levels) if level not in order]
    for level in order:
        front_loads[level].start()

    def halo(slot, source, target, device):
        return pltpu.make_async_remote_copy(
            src_ref=source,
            dst_ref=target,
            send_sem=halo_send.at[slot],
            recv_sem=halo_recv.at[slot],
            device_id=device,
            device_id_type=MESH,
        )

    def chunk_rows(chunk):
        return pl.ds(chunk * rows_per, rows_per)

    edge_halos = [
        halo(0, last_row.at[:, pl.ds(width - LANES, LANES)], edge_left, right),
        halo(1, last_row.at[:, pl.ds(0, LANES)], edge_right, left),
    ]
    rim_halos = [
        halo(2, rim_last, rim_left, right),
        halo(3, rim_first, rim_right, left),
    ]
    above_halo = halo(4, last_row, above, down)
    below_halos = [
        halo(5 + chunk, first_row.at[chunk_rows(chunk)], below.at[chunk_rows(chunk)], up)
        for chunk in range(CHUNKS)
    ]

    def bulk(pair, piece):
        part = pl.ds(piece * PIECE, PIECE)
        return pltpu.make_async_remote_copy(
            src_ref=bulk_out.at[pair, part],
            dst_ref=bulk_in.at[pair, part],
            send_sem=bulk_send.at[pair, piece],
            recv_sem=bulk_recv.at[pair, piece],
            device_id=flip((pairs[pair][1],)),
            device_id_type=MESH,
        )

    def bulk_start(pair, piece):
        part = pl.ds(piece * PIECE, PIECE)
        bulk_out[pair, part] = weights[pairs[pair][0], part].astype(jnp.float32)
        bulk(pair, piece).start()

    def bulk_take(pair, piece):
        part = pl.ds(piece * PIECE, PIECE)
        bulk(pair, piece).wait_recv()
        extra[pair, part] = bulk_in[pair, part].astype(jnp.bfloat16)

    loads[0].wait()
    first_row[...] = cells[:, 0, :]
    last_row[...] = cells[:, depth - 1, :]
    pl.semaphore_wait(barrier, len(friends))
    for copy in edge_halos + below_halos:
        copy.start()
    tell(1)
    above_halo.start()

    rim_lane = lax.broadcasted_iota(jnp.int32, (depth, LANES), 1)
    firsts = jnp.zeros((depth, LANES), jnp.float32)
    lasts = jnp.zeros((depth, LANES), jnp.float32)
    for k in range(k_count):
        head = cells[k, :, pl.ds(0, LANES)]
        tail = cells[k, :, pl.ds(width - LANES, LANES)]
        firsts = jnp.where(rim_lane == k, pltpu.roll(head, k, 1) if k else head, firsts)
        lasts = jnp.where(rim_lane == k, pltpu.roll(tail, k + 1, 1), lasts)
    rim_first[...] = firsts
    rim_last[...] = lasts
    for copy in rim_halos:
        copy.start()

    has_above = (row > 0).astype(jnp.float32)
    has_below = (row < n_row - 1).astype(jnp.float32)
    has_left = (col > 0).astype(jnp.float32)
    has_right = (col < n_col - 1).astype(jnp.float32)

    def beside(block, right_edge, left_edge):
        lane = lax.broadcasted_iota(jnp.int32, block.shape, 1)
        from_right = jnp.where(lane == width - 1, right_edge, pltpu.roll(block, width - 1, 1))
        from_left = jnp.where(lane == 0, left_edge, pltpu.roll(block, 1, 1))
        return from_right, from_left

    def times(state, front):
        return lax.dot_general(
            state.astype(jnp.bfloat16),
            front,
            (((1,), (0,)), ((), ())),
            preferred_element_type=jnp.float32,
        )

    def times_t(state, front):
        return lax.dot_general(
            state.astype(jnp.bfloat16),
            front,
            (((1,), (1,)), ((), ())),
            preferred_element_type=jnp.float32,
        )

    def exchange(phase, slot, chunk):
        part = chunk_rows(chunk)
        return pltpu.make_async_remote_copy(
            src_ref=sent.at[phase, part],
            dst_ref=got.at[phase, slot, part],
            send_sem=send_sem.at[phase, slot, chunk],
            recv_sem=recv_sem.at[phase, slot, chunk],
            device_id=flip(targets[phase][slot]),
            device_id_type=MESH,
        )

    def send(phase, chunk, value):
        sent[phase, chunk_rows(chunk)] = value
        for slot in range(len(targets[phase])):
            exchange(phase, slot, chunk).start()

    def receive(phase, chunk):
        values = []
        for slot in range(len(targets[phase])):
            exchange(phase, slot, chunk).wait_recv()
            values.append(got[phase, slot, chunk_rows(chunk)])
        return values

    def piece(k):
        block = cells[k]
        line = lax.broadcasted_iota(jnp.int32, block.shape, 0)
        under = jnp.where(
            line == depth - 1, below[pl.ds(k, 1), :] * has_below, pltpu.roll(block, depth - 1, 0)
        )
        over = jnp.where(line == 0, above[pl.ds(k, 1), :] * has_above, pltpu.roll(block, 1, 0))
        from_right, from_left = beside(
            block,
            rim_right[:, pl.ds(k, 1)] * has_right,
            rim_left[:, pl.ds(k, 1)] * has_left,
        )
        near = under + over + from_right + from_left
        residual[k] = sources[k] - ((4.0 + shift[...]) * block - near)

    work = [[] for _ in range(phases)]

    def plan(first, last, tasks):
        spots = list(range(max(0, first), min(last, phases - 1) + 1))
        for index, task in enumerate(tasks):
            work[spots[index * len(spots) // len(tasks)]].append(task)

    early = []
    for number, (a, b) in enumerate(pairs):
        starts = [functools.partial(bulk_start, number, p) for p in range(piece_count)]
        takes = [functools.partial(bulk_take, number, p) for p in range(piece_count)]
        use = [at for at in range(levels - 1, phases) if groups[at - levels + 1] == (a, b)][0]
        if number == 0 and a >= col_bits:
            early += starts[:5]
            plan(0, levels - 3, starts[5:])
            plan(levels - 2, levels - 1, takes)
        elif a >= 2:
            early += starts[:4]
            plan(0, 1, starts[4:8])
            plan(col_bits, use - 2, starts[8:])
            plan(use, use, takes)
        else:
            plan(2, use - 1, starts)
            plan(use, use, takes)
    plan(2, phases - 1, [functools.partial(piece, k) for k in range(k_count)])

    def fill(phase, chunk):
        tasks = work[phase]
        for index, task in enumerate(tasks):
            if index * CHUNKS // len(tasks) == chunk:
                task()

    for a, b in pairs:
        front_loads[a].wait()
    for task in early:
        task()

    loads[1].wait()
    loads[2].wait()
    front_loads[0].wait()
    shift_last = shift[pl.ds(depth - 1, 1), :]
    for copy in edge_halos:
        copy.wait_recv()
    for chunk in range(CHUNKS):
        part = chunk_rows(chunk)
        block = last_row[part, :]
        from_right, from_left = beside(
            block,
            edge_right[part, pl.ds(0, 1)] * has_right,
            edge_left[part, pl.ds(LANES - 1, 1)] * has_left,
        )
        below_halos[chunk].wait_recv()
        near = below[part, :] * has_below + cells[part, depth - 2, :] + from_right + from_left
        state = sources[part, depth - 1, :] - ((4.0 + shift_last) * block - near)
        send(0, chunk, times(state, weights[0]))
        fill(0, chunk)

    waited = [0] + [a for a, b in pairs]
    for level in range(1, levels):
        if level not in waited:
            front_loads[level].wait()
        hear(level)
        tell(level + 1)
        if level == 1:
            above_halo.wait_recv()
            for copy in rim_halos:
                copy.wait_recv()
        for chunk in range(CHUNKS):
            (other,) = receive(level - 1, chunk)
            state = other + sign(level - 1) * sent[level - 1, chunk_rows(chunk)]
            send(level, chunk, times(state, weights[level]))
            fill(level, chunk)

    for number, group in enumerate(groups):
        phase = levels - 1 + number
        if len(group) == 2:
            a, b = group
            spare = pairs.index(group)
        for chunk in range(CHUNKS):
            part = chunk_rows(chunk)
            values = receive(phase, chunk)
            mine = sent[phase, part]
            if len(group) == 1:
                mix = 2.0 * values[0] if number == 0 else mine - sign(group[0]) * values[0]
                product = times_t(mix, weights[group[0]])
            else:
                if number == 0:
                    here = 2.0 * values[0]
                    there = 2.0 * values[1]
                else:
                    here = mine - sign(a) * values[0]
                    there = values[1] - sign(a) * values[2]
                here = times_t(here, weights[a])
                there = times_t(there, extra[spare])
                product = times_t(here - sign(b) * there, weights[b])
            if phase + 1 < phases:
                send(phase + 1, chunk, product)
                fill(phase + 1, chunk)
            else:
                separator[part, :] = product

    for copy in edge_halos + rim_halos + [above_halo] + below_halos:
        copy.wait_send()
    for pair in range(len(pairs)):
        for number in range(piece_count):
            bulk(pair, number).wait_send()
    for phase in range(phases):
        for slot in range(len(targets[phase])):
            for chunk in range(CHUNKS):
                exchange(phase, slot, chunk).wait_send()


def body(field, right_side, kappa, fronts):
    k_count, depth, width = field.shape
    n_row = lax.axis_size("row")
    n_col = lax.axis_size("col")
    col_bits = n_col.bit_length() - 1
    levels = col_bits + n_row.bit_length() - 1
    groups, targets = phase_plan(levels, col_bits)
    phases = len(targets)
    slots = max(len(target) for target in targets)
    pairs = sum(len(group) == 2 for group in groups)
    f32 = jnp.float32
    dma = pltpu.SemaphoreType.DMA
    regular = pltpu.SemaphoreType.REGULAR
    cube = pltpu.VMEM((k_count, depth, width), f32)
    line = pltpu.VMEM((k_count, width), f32)
    edge = pltpu.VMEM((k_count, LANES), f32)
    rim = pltpu.VMEM((depth, LANES), f32)
    arrays = (field, right_side, kappa, fronts)
    return pl.pallas_call(
        functools.partial(kernel, (k_count, depth, width, levels, col_bits, n_row, n_col)),
        out_shape=(
            jax.ShapeDtypeStruct((k_count, depth, width), f32),
            jax.ShapeDtypeStruct((k_count, width), f32),
        ),
        in_specs=[pl.BlockSpec(memory_space=pl.ANY)] * 4,
        out_specs=(pl.BlockSpec(memory_space=pltpu.VMEM),) * 2,
        scratch_shapes=[
            cube,
            cube,
            pltpu.VMEM((depth, width), f32),
            pltpu.VMEM((levels, width, width), jnp.bfloat16),
            pltpu.VMEM((pairs, width, width), jnp.bfloat16),
            pltpu.VMEM((pairs, width, width), f32),
            pltpu.VMEM((pairs, width, width), f32),
            line, line, line, line,
            edge, edge,
            rim, rim, rim, rim,
            pltpu.VMEM((phases, k_count, width), f32),
            pltpu.VMEM((phases, slots, k_count, width), f32),
            dma((3,)),
            dma((levels,)),
            dma((5 + CHUNKS,)),
            dma((5 + CHUNKS,)),
            dma((phases, slots, CHUNKS)),
            dma((phases, slots, CHUNKS)),
            dma((pairs, width // PIECE)),
            dma((pairs, width // PIECE)),
            regular((col_bits, 2)),
            regular((levels - col_bits, 2)),
        ],
        compiler_params=pltpu.CompilerParams(
            collective_id=0, has_side_effects=True, vmem_limit_bytes=40 << 20
        ),
    )(*(pltpu.with_memory_space_constraint(array, pltpu.HBM) for array in arrays))


def solution(mesh):
    placed = (P(None, "row", "col"), P(None, "row", "col"), P("row", "col"), P(None, "row", "col"))
    return jax.shard_map(
        body,
        mesh=mesh,
        in_specs=placed,
        out_specs=(P(None, "row", "col"), P("row", "col")),
        check_vma=False,
    )
```

```python
import functools

import jax
import jax.numpy as jnp
from jax import lax
from jax.experimental import pallas as pl
from jax.experimental.pallas import tpu as pltpu
from jax.sharding import PartitionSpec as P

MESH = pl.DeviceIdType.MESH
LANES = 128
CHUNKS = 4
PIECE = 32


def back_groups(levels, col_bits):
    groups = []
    level = levels - 1
    while level >= 0:
        row_pair = level == levels - 1 and level - 1 >= col_bits
        col_pair = level % 2 == 1 and level < col_bits and level <= 3
        if row_pair or col_pair:
            groups.append((level, level - 1))
            level -= 2
        else:
            groups.append((level,))
            level -= 1
    return groups


def group_targets(group, top):
    if len(group) == 1:
        return [group]
    a, b = group
    return [(a,), (a, b)] if top else [(a,), (b,), (a, b)]


def phase_plan(levels, col_bits):
    groups = back_groups(levels, col_bits)
    targets = [group_targets(groups[0], True)]
    for group in groups[1:]:
        targets.append(group_targets(group, False))
    return groups, targets


def kernel(
    sizes,
    field, right_side, kappa, fronts,
    residual, separator,
    cells, sources, shift, weights, turned, extra, bulk_out, bulk_in,
    first_row, last_row, below, above, edge_left, edge_right,
    rim_first, rim_last, rim_left, rim_right,
    sent, got, level_zero, first_got, pair_sent, pair_got, top_sent, hop_out, hop_in, twin,
    load_sem, front_sem, halo_send, halo_recv, send_sem, recv_sem, bulk_send, bulk_recv,
    col_ready, row_ready, first_send, first_recv, pair_send, pair_recv, hop_send, hop_recv,
):
    k_count, depth, width, levels, col_bits, n_row, n_col = sizes
    row = lax.axis_index("row")
    col = lax.axis_index("col")
    rows_per = k_count // CHUNKS
    groups, targets = phase_plan(levels, col_bits)
    phases = len(targets)
    pairs = [group for group in groups if len(group) == 2]
    row_bits = levels - col_bits
    piece_count = width // PIECE

    def flip(toggled):
        if toggled[0] < col_bits:
            return {"col": jnp.bitwise_xor(col, sum(1 << level for level in toggled))}
        return {"row": jnp.bitwise_xor(row, sum(1 << (level - col_bits) for level in toggled))}

    def sign(level):
        place = col if level < col_bits else row
        bit = level if level < col_bits else level - col_bits
        upper = jnp.bitwise_and(jnp.right_shift(place, bit), 1)
        return 1.0 - 2.0 * upper.astype(jnp.float32)

    def row_at(step):
        return {"row": lax.rem(row + (n_row + step) % n_row, n_row)}

    def col_at(step):
        return {"col": lax.rem(col + (n_col + step) % n_col, n_col)}

    up, down, left, right = row_at(-1), row_at(1), col_at(-1), col_at(1)

    barrier = pltpu.get_barrier_semaphore()
    core = lax.rem(row, 2)
    other_core = {"row": jnp.bitwise_xor(row, 1)}
    across = {"row": jnp.bitwise_xor(row, 1), "col": jnp.bitwise_xor(col, 1)}
    friends = [up, down, left, right, across] + [flip((b,)) for a, b in pairs]
    for friend in friends:
        pl.semaphore_signal(barrier, inc=1, device_id=friend, device_id_type=MESH)

    def tell(step):
        for ready, at, bits in ((col_ready, col_at, col_bits), (row_ready, row_at, row_bits)):
            if step < bits:
                for way, sense in ((0, 1), (1, -1)):
                    pl.semaphore_signal(
                        ready.at[step, way],
                        inc=1,
                        device_id=at(sense * (1 << (step - 1))),
                        device_id_type=MESH,
                    )

    def hear(step):
        for ready, bits in ((col_ready, col_bits), (row_ready, row_bits)):
            if step < bits:
                for way in range(2):
                    pl.semaphore_wait(ready.at[step, way], 1)

    loads = [
        pltpu.make_async_copy(field, cells, load_sem.at[0]),
        pltpu.make_async_copy(right_side, sources, load_sem.at[1]),
        pltpu.make_async_copy(kappa, shift, load_sem.at[2]),
    ]
    front_loads = [
        pltpu.make_async_copy(fronts.at[level], weights.at[level], front_sem.at[level])
        for level in range(levels)
    ]
    loads[0].start()
    front_loads[0].start()
    loads[1].start()
    loads[2].start()
    order = [1] + [a for a, b in pairs if a != 1]
    order += [level for level in range(1, levels) if level not in order]
    for level in order:
        front_loads[level].start()

    def halo(slot, source, target, device):
        return pltpu.make_async_remote_copy(
            src_ref=source,
            dst_ref=target,
            send_sem=halo_send.at[slot],
            recv_sem=halo_recv.at[slot],
            device_id=device,
            device_id_type=MESH,
        )

    def chunk_rows(chunk):
        return pl.ds(chunk * rows_per, rows_per)

    edge_halos = [
        halo(0, last_row.at[:, pl.ds(width - LANES, LANES)], edge_left, right),
        halo(1, last_row.at[:, pl.ds(0, LANES)], edge_right, left),
    ]
    rim_halos = [
        halo(2, rim_last, rim_left, right),
        halo(3, rim_first, rim_right, left),
    ]
    above_halo = halo(4, last_row, above, down)
    below_halos = [
        halo(5 + chunk, first_row.at[chunk_rows(chunk)], below.at[chunk_rows(chunk)], up)
        for chunk in range(CHUNKS)
    ]

    def bulk(pair, piece):
        part = pl.ds(piece * PIECE, PIECE)
        return pltpu.make_async_remote_copy(
            src_ref=bulk_out.at[pair, part],
            dst_ref=bulk_in.at[pair, part],
            send_sem=bulk_send.at[pair, piece],
            recv_sem=bulk_recv.at[pair, piece],
            device_id=flip((pairs[pair][1],)),
            device_id_type=MESH,
        )

    def bulk_start(pair, piece):
        part = pl.ds(piece * PIECE, PIECE)
        bulk_out[pair, part] = turned[pairs[pair][0], part].astype(jnp.float32)
        bulk(pair, piece).start()

    def bulk_take(pair, piece):
        part = pl.ds(piece * PIECE, PIECE)
        bulk(pair, piece).wait_recv()
        extra[pair, part] = bulk_in[pair, part].astype(jnp.bfloat16)

    def turn(level, block):
        part = pl.ds(block * LANES, LANES)
        turned[level, part, :] = weights[level, :, part].T

    loads[0].wait()
    first_row[...] = cells[:, 0, :]
    last_row[...] = cells[:, depth - 1, :]
    pl.semaphore_wait(barrier, len(friends))
    for copy in edge_halos + below_halos:
        copy.start()
    tell(1)
    above_halo.start()

    rim_lane = lax.broadcasted_iota(jnp.int32, (depth, LANES), 1)
    firsts = jnp.zeros((depth, LANES), jnp.float32)
    lasts = jnp.zeros((depth, LANES), jnp.float32)
    for k in range(k_count):
        head = cells[k, :, pl.ds(0, LANES)]
        tail = cells[k, :, pl.ds(width - LANES, LANES)]
        firsts = jnp.where(rim_lane == k, pltpu.roll(head, k, 1) if k else head, firsts)
        lasts = jnp.where(rim_lane == k, pltpu.roll(tail, k + 1, 1), lasts)
    rim_first[...] = firsts
    rim_last[...] = lasts
    for copy in rim_halos:
        copy.start()

    has_above = (row > 0).astype(jnp.float32)
    has_below = (row < n_row - 1).astype(jnp.float32)
    has_left = (col > 0).astype(jnp.float32)
    has_right = (col < n_col - 1).astype(jnp.float32)

    def beside(block, right_edge, left_edge):
        lane = lax.broadcasted_iota(jnp.int32, block.shape, 1)
        from_right = jnp.where(lane == width - 1, right_edge, pltpu.roll(block, width - 1, 1))
        from_left = jnp.where(lane == 0, left_edge, pltpu.roll(block, 1, 1))
        return from_right, from_left

    def times(state, front):
        return lax.dot_general(
            state.astype(jnp.bfloat16),
            front,
            (((1,), (0,)), ((), ())),
            preferred_element_type=jnp.float32,
        )

    def exchange(phase, slot, chunk):
        part = chunk_rows(chunk)
        return pltpu.make_async_remote_copy(
            src_ref=sent.at[phase, part],
            dst_ref=got.at[phase, slot, part],
            send_sem=send_sem.at[phase, slot, chunk],
            recv_sem=recv_sem.at[phase, slot, chunk],
            device_id=flip(targets[phase][slot]),
            device_id_type=MESH,
        )

    def send(phase, chunk, value):
        sent[phase, chunk_rows(chunk)] = value
        for slot in range(len(targets[phase])):
            exchange(phase, slot, chunk).start()

    def receive(phase, chunk):
        values = []
        for slot in range(len(targets[phase])):
            exchange(phase, slot, chunk).wait_recv()
            values.append(got[phase, slot, chunk_rows(chunk)])
        return values

    def piece(k):
        block = cells[k]
        line = lax.broadcasted_iota(jnp.int32, block.shape, 0)
        under = jnp.where(
            line == depth - 1, below[pl.ds(k, 1), :] * has_below, pltpu.roll(block, depth - 1, 0)
        )
        over = jnp.where(line == 0, above[pl.ds(k, 1), :] * has_above, pltpu.roll(block, 1, 0))
        from_right, from_left = beside(
            block,
            rim_right[:, pl.ds(k, 1)] * has_right,
            rim_left[:, pl.ds(k, 1)] * has_left,
        )
        near = under + over + from_right + from_left
        residual[k] = sources[k] - ((4.0 + shift[...]) * block - near)

    top_level = levels - 1
    local = col_bits

    def first(slot, chunk):
        part = chunk_rows(chunk)
        return pltpu.make_async_remote_copy(
            src_ref=level_zero.at[part],
            dst_ref=first_got.at[slot, part],
            send_sem=first_send.at[slot, chunk],
            recv_sem=first_recv.at[slot, chunk],
            device_id=(other_core, across, flip((0,)))[slot],
            device_id_type=MESH,
        )

    def pair_copy(level, chunk):
        return pltpu.make_async_remote_copy(
            src_ref=pair_sent.at[level, chunk],
            dst_ref=pair_got.at[level, chunk],
            send_sem=pair_send.at[level, chunk],
            recv_sem=pair_recv.at[level, chunk],
            device_id=flip((level,)),
            device_id_type=MESH,
        )

    def top_copy(owner, slot, chunk):
        part = chunk_rows(chunk)
        steps = sum(1 << (level - col_bits) for level in targets[0][slot])
        return pltpu.make_async_remote_copy(
            src_ref=top_sent.at[owner, part],
            dst_ref=got.at[0, slot, part],
            send_sem=send_sem.at[0, slot, owner * CHUNKS + chunk],
            recv_sem=recv_sem.at[0, slot, chunk],
            device_id={"row": jnp.bitwise_xor(row, steps + 1 - owner)},
            device_id_type=MESH,
        )

    hop_pieces = width // LANES

    def hop(level, piece):
        part = pl.ds(piece * LANES, LANES)
        return pltpu.make_async_remote_copy(
            src_ref=hop_out.at[level % 2, part],
            dst_ref=hop_in.at[level, part],
            send_sem=hop_send.at[level, piece],
            recv_sem=hop_recv.at[level, piece],
            device_id=other_core,
            device_id_type=MESH,
        )

    def hop_start(level):
        for number in range(hop_pieces):
            part = pl.ds(number * LANES, LANES)
            hop_out[level % 2, part] = weights[level, part].astype(jnp.float32)
            hop(level, number).start()

    def hop_sent(level):
        for number in range(hop_pieces):
            hop(level, number).wait_send()

    def hop_take(level):
        for number in range(hop_pieces):
            part = pl.ds(number * LANES, LANES)
            hop(level, number).wait_recv()
            twin[level, part] = hop_in[level, part].astype(jnp.bfloat16)

    def spread(tasks, spots):
        out = [[] for _ in range(spots)]
        for index, task in enumerate(tasks):
            out[index * spots // len(tasks)].append(task)
        return out

    starts = []
    takes = []
    for number in range(len(pairs)):
        starts.append([functools.partial(bulk_start, number, p) for p in range(piece_count)])
        takes.append([functools.partial(bulk_take, number, p) for p in range(piece_count)])
    blocks = width // LANES
    ready_turns = [a for a, b in pairs if a != 1]
    early = []
    for number, (a, b) in enumerate(pairs):
        if a != 1:
            quick = 5 if a >= col_bits else 4
            early += starts[number][:quick]
            starts[number] = starts[number][quick:]
    late_turns = [
        [functools.partial(turn, level, block) for block in range(blocks)]
        for level in range(levels)
        if level not in ready_turns and level != 1
    ]
    residual_tasks = [functools.partial(piece, k) for k in range(k_count)]

    front_loads[1].wait()

    @pl.when(core == 0)
    def _():
        hop_start(1)

    for a, b in pairs:
        if a != 1:
            front_loads[a].wait()
            for block in range(blocks):
                turn(a, block)
    for task in early:
        task()

    loads[1].wait()
    loads[2].wait()
    front_loads[0].wait()
    shift_last = shift[pl.ds(depth - 1, 1), :]
    for copy in edge_halos:
        copy.wait_recv()
    for chunk in range(CHUNKS):
        part = chunk_rows(chunk)
        block = last_row[part, :]
        from_right, from_left = beside(
            block,
            edge_right[part, pl.ds(0, 1)] * has_right,
            edge_left[part, pl.ds(LANES - 1, 1)] * has_left,
        )
        below_halos[chunk].wait_recv()
        near = below[part, :] * has_below + cells[part, depth - 2, :] + from_right + from_left
        state = sources[part, depth - 1, :] - ((4.0 + shift_last) * block - near)
        product = times(state, weights[0])
        level_zero[part, :] = product

        @pl.when(core == 0)
        def _():
            first(1, chunk).start()
            first(0, chunk).start()

        @pl.when(core == 1)
        def _():
            first(2, chunk).start()

    for level in range(2, levels):
        if level not in ready_turns:
            front_loads[level].wait()
    above_halo.wait_recv()
    for copy in rim_halos:
        copy.wait_recv()

    @pl.when(core == 0)
    def _():
        for level in range(1, levels):
            hear(level)
            tell(level + 1)
        steps = list(range(2, levels))
        plans = [[] for _ in steps]
        rest = []
        for number, (a, b) in enumerate(pairs):
            if a >= col_bits:
                for at, tasks in enumerate(spread(starts[number], len(steps))):
                    plans[at] += tasks
            elif a != 1:
                rest += starts[number]
            else:
                rest = [functools.partial(turn, 1, block) for block in range(blocks)] + rest + starts[number]
        for at, tasks in enumerate(spread(sum(late_turns, []) + residual_tasks, len(steps))):
            plans[at] += tasks
        for at, level in enumerate(steps):
            if level >= 3:
                hop_sent(level - 2)
            hop_start(level)
            for task in plans[at]:
                task()
        for task in rest:
            task()
        if pairs[0][0] >= col_bits:
            for task in takes[0]:
                task()
        for level in range(max(1, levels - 2), levels):
            hop_sent(level)
        for slot in range(2):
            for chunk in range(CHUNKS):
                first(slot, chunk).wait_send()

    @pl.when(core == 1)
    def _():
        stages = [level for level in range(1, levels) if level != local + 1]
        plans = [[] for _ in stages]

        def add(first_level, last_level, tasks):
            spots = [at for at, level in enumerate(stages) if first_level <= level <= last_level]
            spots = spots or [len(stages) - 1]
            for at, part in zip(spots, spread(tasks, len(spots))):
                plans[at] += part

        for number, (a, b) in enumerate(pairs):
            if a >= col_bits:
                add(1, levels - 2, starts[number])
                add(levels - 1, levels - 1, takes[number])
            elif a != 1:
                add(1, 1, starts[number][:4])
                add(local, levels - 1, starts[number][4:])
            else:
                add(1, 1, [functools.partial(turn, 1, block) for block in range(blocks)])
                add(2, levels - 1, starts[number])
        for at, tasks in enumerate(late_turns):
            add(2 + at, 2 + at, tasks)
        add(2, levels - 1, residual_tasks[:k_count // 2])

        def fill(tasks, chunk):
            for index, task in enumerate(tasks):
                if index * CHUNKS // len(tasks) == chunk:
                    task()

        hop_take(1)
        for at, level in enumerate(stages):
            hear(level)
            tell(level + 1)
            if level == local:
                hear(level + 1)
                tell(level + 2)
            for chunk in range(CHUNKS):
                part = chunk_rows(chunk)
                sense = sign(level - 1)
                if level == 1:
                    for slot in range(3):
                        first(slot, chunk).wait_recv()
                    low = first_got[1, part] + sense * first_got[0, part]
                    high = first_got[2, part] + sense * level_zero[part, :]
                else:
                    past = level - 1
                    pair_copy(past, chunk).wait_recv()
                    both = pair_got[past, chunk] + sense * pair_sent[past, chunk]
                    low = both[:rows_per]
                    high = both[rows_per:]
                low = times(low, twin[level])
                high = times(high, weights[level])
                out = level
                if level == local:
                    low, high = low + high, low - high
                    out = level + 1
                    low = times(low, twin[out])
                    high = times(high, weights[out])
                if out == top_level:
                    for owner, value in enumerate((low, high)):
                        top_sent[owner, part] = value
                        for slot in range(len(targets[0])):
                            top_copy(owner, slot, chunk).start()
                else:
                    pair_sent[out, chunk, pl.ds(0, rows_per)] = low
                    pair_sent[out, chunk, pl.ds(rows_per, rows_per)] = high
                    pair_copy(out, chunk).start()
                fill(plans[at], chunk)
            if out < top_level:
                hop_take(out + 1)
                if out + 1 == local:
                    hop_take(out + 2)
        for chunk in range(CHUNKS):
            first(2, chunk).wait_send()
            for level in range(1, top_level):
                if level != local:
                    pair_copy(level, chunk).wait_send()
            for owner in range(2):
                for slot in range(len(targets[0])):
                    top_copy(owner, slot, chunk).wait_send()

    work = [[] for _ in range(phases)]
    for number, (a, b) in enumerate(pairs):
        if a < col_bits:
            work[groups.index((a, b))] += takes[number]

    def fill_back(phase, chunk):
        tasks = work[phase]
        for index, task in enumerate(tasks):
            if index * CHUNKS // len(tasks) == chunk:
                task()

        @pl.when(core == 1)
        def _():
            later = residual_tasks[k_count // 2:]
            for index, task in enumerate(later):
                if index * (phases - 1) * CHUNKS // len(later) == (phase - 1) * CHUNKS + chunk:
                    task()

    for number, group in enumerate(groups):
        phase = number
        if len(group) == 2:
            a, b = group
            spare = pairs.index(group)
        for chunk in range(CHUNKS):
            part = chunk_rows(chunk)
            values = receive(phase, chunk)
            mine = sent[phase, part] if number else None
            if len(group) == 1:
                mix = 2.0 * values[0] if number == 0 else mine - sign(group[0]) * values[0]
                product = times(mix, turned[group[0]])
            else:
                if number == 0:
                    here = 2.0 * values[0]
                    there = 2.0 * values[1]
                else:
                    here = mine - sign(a) * values[0]
                    there = values[1] - sign(a) * values[2]
                here = times(here, turned[a])
                there = times(there, extra[spare])
                product = times(here - sign(b) * there, turned[b])
            if phase + 1 < phases:
                send(phase + 1, chunk, product)
                fill_back(phase + 1, chunk)
            else:
                separator[part, :] = product

    for copy in edge_halos + rim_halos + [above_halo] + below_halos:
        copy.wait_send()
    for pair in range(len(pairs)):
        for number in range(piece_count):
            bulk(pair, number).wait_send()
    for phase in range(1, phases):
        for slot in range(len(targets[phase])):
            for chunk in range(CHUNKS):
                exchange(phase, slot, chunk).wait_send()


def body(field, right_side, kappa, fronts):
    k_count, depth, width = field.shape
    n_row = lax.axis_size("row")
    n_col = lax.axis_size("col")
    col_bits = n_col.bit_length() - 1
    levels = col_bits + n_row.bit_length() - 1
    groups, targets = phase_plan(levels, col_bits)
    phases = len(targets)
    slots = max(len(target) for target in targets)
    pairs = sum(len(group) == 2 for group in groups)
    f32 = jnp.float32
    dma = pltpu.SemaphoreType.DMA
    regular = pltpu.SemaphoreType.REGULAR
    cube = pltpu.VMEM((k_count, depth, width), f32)
    line = pltpu.VMEM((k_count, width), f32)
    edge = pltpu.VMEM((k_count, LANES), f32)
    rim = pltpu.VMEM((depth, LANES), f32)
    arrays = (field, right_side, kappa, fronts)
    return pl.pallas_call(
        functools.partial(kernel, (k_count, depth, width, levels, col_bits, n_row, n_col)),
        out_shape=(
            jax.ShapeDtypeStruct((k_count, depth, width), f32),
            jax.ShapeDtypeStruct((k_count, width), f32),
        ),
        in_specs=[pl.BlockSpec(memory_space=pl.ANY)] * 4,
        out_specs=(pl.BlockSpec(memory_space=pltpu.VMEM),) * 2,
        scratch_shapes=[
            cube,
            cube,
            pltpu.VMEM((depth, width), f32),
            pltpu.VMEM((levels, width, width), jnp.bfloat16),
            pltpu.VMEM((levels, width, width), jnp.bfloat16),
            pltpu.VMEM((pairs, width, width), jnp.bfloat16),
            pltpu.VMEM((pairs, width, width), f32),
            pltpu.VMEM((pairs, width, width), f32),
            line, line, line, line,
            edge, edge,
            rim, rim, rim, rim,
            pltpu.VMEM((phases, k_count, width), f32),
            pltpu.VMEM((phases, slots, k_count, width), f32),
            line,
            pltpu.VMEM((3, k_count, width), f32),
            pltpu.VMEM((levels, CHUNKS, 2 * k_count // CHUNKS, width), f32),
            pltpu.VMEM((levels, CHUNKS, 2 * k_count // CHUNKS, width), f32),
            pltpu.VMEM((2, k_count, width), f32),
            pltpu.VMEM((2, width, width), f32),
            pltpu.VMEM((levels, width, width), f32),
            pltpu.VMEM((levels, width, width), jnp.bfloat16),
            dma((3,)),
            dma((levels,)),
            dma((5 + CHUNKS,)),
            dma((5 + CHUNKS,)),
            dma((phases, slots, 2 * CHUNKS)),
            dma((phases, slots, CHUNKS)),
            dma((pairs, width // PIECE)),
            dma((pairs, width // PIECE)),
            regular((col_bits, 2)),
            regular((levels - col_bits, 2)),
            dma((3, CHUNKS)),
            dma((3, CHUNKS)),
            dma((levels, CHUNKS)),
            dma((levels, CHUNKS)),
            dma((levels, width // LANES)),
            dma((levels, width // LANES)),
        ],
        compiler_params=pltpu.CompilerParams(
            collective_id=0, has_side_effects=True, vmem_limit_bytes=48 << 20
        ),
    )(*(pltpu.with_memory_space_constraint(array, pltpu.HBM) for array in arrays))


def solution(mesh):
    placed = (P(None, "row", "col"), P(None, "row", "col"), P("row", "col"), P(None, "row", "col"))
    return jax.shard_map(
        body,
        mesh=mesh,
        in_specs=placed,
        out_specs=(P(None, "row", "col"), P("row", "col")),
        check_vma=False,
    )
```

```python
import functools

import jax
import jax.numpy as jnp
from jax import lax
from jax.experimental import pallas as pl
from jax.experimental.pallas import tpu as pltpu
from jax.sharding import PartitionSpec as P

MESH = pl.DeviceIdType.MESH
LANES = 128
CHUNKS = 2
HOP_SLOTS = 4
X_STEP = 1
Y_EARLY = 16
PIECE = 32


def back_groups(levels, col_bits):
    groups = []
    level = levels - 1
    while level >= 0:
        row_pair = level == levels - 1 and level - 1 >= col_bits
        col_pair = level % 2 == 1 and level < col_bits and level <= 1
        if row_pair or col_pair:
            groups.append((level, level - 1))
            level -= 2
        else:
            groups.append((level,))
            level -= 1
    return groups


def group_targets(group, top):
    if len(group) == 1:
        return [group]
    a, b = group
    return [(a,), (a, b)] if top else [(a,), (b,), (a, b)]


def phase_plan(levels, col_bits):
    groups = back_groups(levels, col_bits)
    targets = [group_targets(groups[0], True)]
    for group in groups[1:]:
        targets.append(group_targets(group, False))
    return groups, targets


def kernel(
    sizes,
    field, right_side, kappa, fronts,
    residual, separator,
    cells, sources, shift, weights, turned, extra, bulk_out, bulk_in,
    first_row, last_row, below, above, edge_left, edge_right,
    rim_first, rim_last, rim_left, rim_right,
    sent, got, level_zero, first_got, pair_sent, pair_got, top_sent, hop_out, hop_in, twin,
    load_sem, front_sem, halo_send, halo_recv, send_sem, recv_sem, bulk_send, bulk_recv,
    col_ready, row_ready, first_send, first_recv, pair_send, pair_recv, hop_send, hop_recv,
):
    k_count, depth, width, levels, col_bits, n_row, n_col = sizes
    row = lax.axis_index("row")
    col = lax.axis_index("col")
    rows_per = k_count // CHUNKS
    groups, targets = phase_plan(levels, col_bits)
    phases = len(targets)
    pairs = [group for group in groups if len(group) == 2]
    row_bits = levels - col_bits
    piece_count = width // PIECE

    def flip(toggled):
        if toggled[0] < col_bits:
            return {"col": jnp.bitwise_xor(col, sum(1 << level for level in toggled))}
        return {"row": jnp.bitwise_xor(row, sum(1 << (level - col_bits) for level in toggled))}

    def sign(level):
        place = col if level < col_bits else row
        bit = level if level < col_bits else level - col_bits
        upper = jnp.bitwise_and(jnp.right_shift(place, bit), 1)
        return 1.0 - 2.0 * upper.astype(jnp.float32)

    def row_at(step):
        return {"row": lax.rem(row + (n_row + step) % n_row, n_row)}

    def col_at(step):
        return {"col": lax.rem(col + (n_col + step) % n_col, n_col)}

    up, down, left, right = row_at(-1), row_at(1), col_at(-1), col_at(1)

    barrier = pltpu.get_barrier_semaphore()
    core = lax.rem(row, 2)
    other_core = {"row": jnp.bitwise_xor(row, 1)}
    across = {"row": jnp.bitwise_xor(row, 1), "col": jnp.bitwise_xor(col, 1)}
    friends = [up, down, left, right, across] + [flip((b,)) for a, b in pairs]
    for friend in friends:
        pl.semaphore_signal(barrier, inc=1, device_id=friend, device_id_type=MESH)

    def tell(step):
        for ready, at, bits in ((col_ready, col_at, col_bits), (row_ready, row_at, row_bits)):
            if step < bits:
                for way, sense in ((0, 1), (1, -1)):
                    pl.semaphore_signal(
                        ready.at[step, way],
                        inc=1,
                        device_id=at(sense * (1 << (step - 1))),
                        device_id_type=MESH,
                    )

    def hear(step):
        for ready, bits in ((col_ready, col_bits), (row_ready, row_bits)):
            if step < bits:
                for way in range(2):
                    pl.semaphore_wait(ready.at[step, way], 1)

    loads = [
        pltpu.make_async_copy(field, cells, load_sem.at[0]),
        pltpu.make_async_copy(right_side, sources, load_sem.at[1]),
        pltpu.make_async_copy(kappa, shift, load_sem.at[2]),
    ]
    front_loads = [
        pltpu.make_async_copy(fronts.at[level], weights.at[level], front_sem.at[level])
        for level in range(levels)
    ]
    loads[0].start()
    front_loads[0].start()
    loads[1].start()
    loads[2].start()
    order = [1, 2] + [a for a, b in pairs if a != 1]
    order += [level for level in range(1, levels) if level not in order]
    for level in order:
        front_loads[level].start()

    def halo(slot, source, target, device):
        return pltpu.make_async_remote_copy(
            src_ref=source,
            dst_ref=target,
            send_sem=halo_send.at[slot],
            recv_sem=halo_recv.at[slot],
            device_id=device,
            device_id_type=MESH,
        )

    def chunk_rows(chunk):
        return pl.ds(chunk * rows_per, rows_per)

    edge_halos = [
        halo(0, last_row.at[:, pl.ds(width - LANES, LANES)], edge_left, right),
        halo(1, last_row.at[:, pl.ds(0, LANES)], edge_right, left),
    ]
    rim_halos = [
        halo(2, rim_last, rim_left, right),
        halo(3, rim_first, rim_right, left),
    ]
    above_halo = halo(4, last_row, above, down)
    below_halos = [
        halo(5 + chunk, first_row.at[chunk_rows(chunk)], below.at[chunk_rows(chunk)], up)
        for chunk in range(CHUNKS)
    ]

    def bulk(pair, piece):
        part = pl.ds(piece * PIECE, PIECE)
        return pltpu.make_async_remote_copy(
            src_ref=bulk_out.at[pair, part],
            dst_ref=bulk_in.at[pair, part],
            send_sem=bulk_send.at[pair, piece],
            recv_sem=bulk_recv.at[pair, piece],
            device_id=flip((pairs[pair][1],)),
            device_id_type=MESH,
        )

    def bulk_start(pair, piece):
        part = pl.ds(piece * PIECE, PIECE)
        bulk_out[pair, part] = turned[pairs[pair][0], part].astype(jnp.float32)
        bulk(pair, piece).start()

    def bulk_take(pair, piece):
        part = pl.ds(piece * PIECE, PIECE)
        bulk(pair, piece).wait_recv()
        extra[pair, part] = bulk_in[pair, part].astype(jnp.bfloat16)

    def turn(level, block):
        part = pl.ds(block * LANES, LANES)
        turned[level, part, :] = weights[level, :, part].T

    loads[0].wait()
    first_row[...] = cells[:, 0, :]
    last_row[...] = cells[:, depth - 1, :]
    pl.semaphore_wait(barrier, len(friends))
    for copy in edge_halos + below_halos:
        copy.start()
    tell(1)
    above_halo.start()

    rim_lane = lax.broadcasted_iota(jnp.int32, (depth, LANES), 1)
    firsts = jnp.zeros((depth, LANES), jnp.float32)
    lasts = jnp.zeros((depth, LANES), jnp.float32)
    for k in range(k_count):
        head = cells[k, :, pl.ds(0, LANES)]
        tail = cells[k, :, pl.ds(width - LANES, LANES)]
        firsts = jnp.where(rim_lane == k, pltpu.roll(head, k, 1) if k else head, firsts)
        lasts = jnp.where(rim_lane == k, pltpu.roll(tail, k + 1, 1), lasts)
    rim_first[...] = firsts
    rim_last[...] = lasts
    for copy in rim_halos:
        copy.start()

    has_above = (row > 0).astype(jnp.float32)
    has_below = (row < n_row - 1).astype(jnp.float32)
    has_left = (col > 0).astype(jnp.float32)
    has_right = (col < n_col - 1).astype(jnp.float32)

    def beside(block, right_edge, left_edge):
        lane = lax.broadcasted_iota(jnp.int32, block.shape, 1)
        from_right = jnp.where(lane == width - 1, right_edge, pltpu.roll(block, width - 1, 1))
        from_left = jnp.where(lane == 0, left_edge, pltpu.roll(block, 1, 1))
        return from_right, from_left

    def times(state, front):
        return lax.dot_general(
            state.astype(jnp.bfloat16),
            front,
            (((1,), (0,)), ((), ())),
            preferred_element_type=jnp.float32,
        )

    def exchange(phase, slot, chunk):
        part = chunk_rows(chunk)
        return pltpu.make_async_remote_copy(
            src_ref=sent.at[phase, part],
            dst_ref=got.at[phase, slot, part],
            send_sem=send_sem.at[phase, slot, chunk],
            recv_sem=recv_sem.at[phase, slot, chunk],
            device_id=flip(targets[phase][slot]),
            device_id_type=MESH,
        )

    def send(phase, chunk, value):
        sent[phase, chunk_rows(chunk)] = value
        for slot in range(len(targets[phase])):
            exchange(phase, slot, chunk).start()

    def receive(phase, chunk):
        values = []
        for slot in range(len(targets[phase])):
            exchange(phase, slot, chunk).wait_recv()
            values.append(got[phase, slot, chunk_rows(chunk)])
        return values

    def piece(k):
        block = cells[k]
        line = lax.broadcasted_iota(jnp.int32, block.shape, 0)
        under = jnp.where(
            line == depth - 1, below[pl.ds(k, 1), :] * has_below, pltpu.roll(block, depth - 1, 0)
        )
        over = jnp.where(line == 0, above[pl.ds(k, 1), :] * has_above, pltpu.roll(block, 1, 0))
        from_right, from_left = beside(
            block,
            rim_right[:, pl.ds(k, 1)] * has_right,
            rim_left[:, pl.ds(k, 1)] * has_left,
        )
        near = under + over + from_right + from_left
        residual[k] = sources[k] - ((4.0 + shift[...]) * block - near)

    top_level = levels - 1
    local = col_bits

    def first(slot, chunk):
        part = chunk_rows(chunk)
        return pltpu.make_async_remote_copy(
            src_ref=level_zero.at[part],
            dst_ref=first_got.at[slot, part],
            send_sem=first_send.at[slot, chunk],
            recv_sem=first_recv.at[slot, chunk],
            device_id=(other_core, across, flip((0,)))[slot],
            device_id_type=MESH,
        )

    def pair_copy(level, chunk):
        return pltpu.make_async_remote_copy(
            src_ref=pair_sent.at[level, chunk],
            dst_ref=pair_got.at[level, chunk],
            send_sem=pair_send.at[level, chunk],
            recv_sem=pair_recv.at[level, chunk],
            device_id=flip((level,)),
            device_id_type=MESH,
        )

    def top_copy(owner, slot, chunk):
        part = chunk_rows(chunk)
        steps = sum(1 << (level - col_bits) for level in targets[0][slot])
        return pltpu.make_async_remote_copy(
            src_ref=top_sent.at[owner, part],
            dst_ref=got.at[0, slot, part],
            send_sem=send_sem.at[0, slot, owner * CHUNKS + chunk],
            recv_sem=recv_sem.at[0, slot, chunk],
            device_id={"row": jnp.bitwise_xor(row, steps + 1 - owner)},
            device_id_type=MESH,
        )

    hop_pieces = width // LANES

    def hop(level, piece):
        part = pl.ds(piece * LANES, LANES)
        return pltpu.make_async_remote_copy(
            src_ref=hop_out.at[level % HOP_SLOTS, part],
            dst_ref=hop_in.at[level, part],
            send_sem=hop_send.at[level, piece],
            recv_sem=hop_recv.at[level, piece],
            device_id=other_core,
            device_id_type=MESH,
        )

    def hop_start(level):
        for number in range(hop_pieces):
            part = pl.ds(number * LANES, LANES)
            hop_out[level % HOP_SLOTS, part] = weights[level, part].astype(jnp.float32)
            hop(level, number).start()

    def hop_sent(level):
        for number in range(hop_pieces):
            hop(level, number).wait_send()

    def hop_take(level):
        for number in range(hop_pieces):
            part = pl.ds(number * LANES, LANES)
            hop(level, number).wait_recv()
            twin[level, part] = hop_in[level, part].astype(jnp.bfloat16)

    def spread(tasks, spots):
        out = [[] for _ in range(spots)]
        for index, task in enumerate(tasks):
            out[index * spots // len(tasks)].append(task)
        return out

    starts = []
    takes = []
    for number in range(len(pairs)):
        starts.append([functools.partial(bulk_start, number, p) for p in range(piece_count)])
        takes.append([functools.partial(bulk_take, number, p) for p in range(piece_count)])
    blocks = width // LANES
    ready_turns = [a for a, b in pairs if a != 1]
    early = []
    for number, (a, b) in enumerate(pairs):
        if a != 1:
            early += starts[number][:Y_EARLY]
            starts[number] = starts[number][Y_EARLY:]
    late_turns = [
        [functools.partial(turn, level, block) for block in range(blocks)]
        for level in range(levels)
        if level not in ready_turns and level != 1
    ]
    residual_tasks = [functools.partial(piece, k) for k in range(k_count)]

    front_loads[1].wait()

    @pl.when(core == 0)
    def _():
        hop_start(1)
        front_loads[2].wait()
        hop_start(2)

    for a, b in pairs:
        if a != 1:
            front_loads[a].wait()
            for block in range(blocks):
                turn(a, block)
    for task in early:
        task()

    loads[1].wait()
    loads[2].wait()
    front_loads[0].wait()
    shift_last = shift[pl.ds(depth - 1, 1), :]
    for copy in edge_halos:
        copy.wait_recv()
    for chunk in range(CHUNKS):
        part = chunk_rows(chunk)
        block = last_row[part, :]
        from_right, from_left = beside(
            block,
            edge_right[part, pl.ds(0, 1)] * has_right,
            edge_left[part, pl.ds(LANES - 1, 1)] * has_left,
        )
        below_halos[chunk].wait_recv()
        near = below[part, :] * has_below + cells[part, depth - 2, :] + from_right + from_left
        state = sources[part, depth - 1, :] - ((4.0 + shift_last) * block - near)
        product = times(state, weights[0])
        level_zero[part, :] = product

        @pl.when(core == 0)
        def _():
            first(1, chunk).start()
            first(0, chunk).start()

        @pl.when(core == 1)
        def _():
            first(2, chunk).start()

    @pl.when(core == 1)
    def _():
        front_loads[2].wait()

    for level in range(3, levels):
        if level not in ready_turns:
            front_loads[level].wait()
    above_halo.wait_recv()
    for copy in rim_halos:
        copy.wait_recv()

    @pl.when(core == 0)
    def _():
        for level in range(1, levels):
            hear(level)
            tell(level + 1)
        steps = list(range(3, levels))
        plans = [[] for _ in steps]
        rest = []

        def add(first_step, tasks):
            spots = len(steps) - min(first_step, len(steps) - 1)
            for at, part in enumerate(spread(tasks, spots)):
                plans[len(steps) - spots + at] += part

        for number, (a, b) in enumerate(pairs):
            if a >= col_bits:
                add(0, starts[number])
            else:
                add(0, [functools.partial(turn, 1, block) for block in range(blocks)])
                add(X_STEP, starts[number])
        for at, tasks in enumerate(spread(sum(late_turns, []) + residual_tasks, len(steps))):
            plans[at] += tasks
        for at, level in enumerate(steps):
            if level > HOP_SLOTS:
                hop_sent(level - HOP_SLOTS)
            hop_start(level)
            for task in plans[at]:
                task()
        for task in rest:
            task()
        if pairs[0][0] >= col_bits:
            for task in takes[0]:
                task()
        for level in range(max(1, levels - HOP_SLOTS), levels):
            hop_sent(level)
        for slot in range(2):
            for chunk in range(CHUNKS):
                first(slot, chunk).wait_send()

    @pl.when(core == 1)
    def _():
        stages = [level for level in range(1, levels) if level != local + 1]
        plans = [[] for _ in stages]

        def add(first_level, last_level, tasks):
            spots = [at for at, level in enumerate(stages) if first_level <= level <= last_level]
            spots = spots or [len(stages) - 1]
            for at, part in zip(spots, spread(tasks, len(spots))):
                plans[at] += part

        for number, (a, b) in enumerate(pairs):
            if a >= col_bits:
                add(1, levels - 2, starts[number])
                add(levels - 1, levels - 1, takes[number])
            else:
                add(1, 1, [functools.partial(turn, 1, block) for block in range(blocks)])
                add(2, levels - 1, starts[number])
        for at, tasks in enumerate(late_turns):
            add(2 + at, 2 + at, tasks)
        add(2, levels - 1, residual_tasks[:k_count // 2])

        def fill(tasks, chunk):
            for index, task in enumerate(tasks):
                if index * CHUNKS // len(tasks) == chunk:
                    task()

        hop_take(1)
        for at, level in enumerate(stages):
            hear(level)
            tell(level + 1)
            if level == local:
                hear(level + 1)
                tell(level + 2)
            for chunk in range(CHUNKS):
                part = chunk_rows(chunk)
                sense = sign(level - 1)
                if level == 1:
                    for slot in range(3):
                        first(slot, chunk).wait_recv()
                    low = first_got[1, part] + sense * first_got[0, part]
                    high = first_got[2, part] + sense * level_zero[part, :]
                else:
                    past = level - 1
                    pair_copy(past, chunk).wait_recv()
                    both = pair_got[past, chunk] + sense * pair_sent[past, chunk]
                    low = both[:rows_per]
                    high = both[rows_per:]
                low = times(low, twin[level])
                high = times(high, weights[level])
                out = level
                if level == local:
                    low, high = low + high, low - high
                    out = level + 1
                    low = times(low, twin[out])
                    high = times(high, weights[out])
                if out == top_level:
                    for owner, value in enumerate((low, high)):
                        top_sent[owner, part] = value
                        for slot in range(len(targets[0])):
                            top_copy(owner, slot, chunk).start()
                else:
                    pair_sent[out, chunk, pl.ds(0, rows_per)] = low
                    pair_sent[out, chunk, pl.ds(rows_per, rows_per)] = high
                    pair_copy(out, chunk).start()
                fill(plans[at], chunk)
            if out < top_level:
                hop_take(out + 1)
                if out + 1 == local:
                    hop_take(out + 2)
        for chunk in range(CHUNKS):
            first(2, chunk).wait_send()
            for level in range(1, top_level):
                if level != local:
                    pair_copy(level, chunk).wait_send()
            for owner in range(2):
                for slot in range(len(targets[0])):
                    top_copy(owner, slot, chunk).wait_send()

    work = [[] for _ in range(phases)]
    for number, (a, b) in enumerate(pairs):
        if a < col_bits:
            work[groups.index((a, b))] += takes[number]

    def fill_back(phase, chunk):
        tasks = work[phase]
        for index, task in enumerate(tasks):
            if index * CHUNKS // len(tasks) == chunk:
                task()

        @pl.when(core == 1)
        def _():
            later = residual_tasks[k_count // 2:]
            for index, task in enumerate(later):
                if index * (phases - 1) * CHUNKS // len(later) == (phase - 1) * CHUNKS + chunk:
                    task()

    for number, group in enumerate(groups):
        phase = number
        if len(group) == 2:
            a, b = group
            spare = pairs.index(group)
        for chunk in range(CHUNKS):
            part = chunk_rows(chunk)
            values = receive(phase, chunk)
            mine = sent[phase, part] if number else None
            if len(group) == 1:
                mix = 2.0 * values[0] if number == 0 else mine - sign(group[0]) * values[0]
                product = times(mix, turned[group[0]])
            else:
                if number == 0:
                    here = 2.0 * values[0]
                    there = 2.0 * values[1]
                else:
                    here = mine - sign(a) * values[0]
                    there = values[1] - sign(a) * values[2]
                here = times(here, turned[a])
                there = times(there, extra[spare])
                product = times(here - sign(b) * there, turned[b])
            if phase + 1 < phases:
                send(phase + 1, chunk, product)
                fill_back(phase + 1, chunk)
            else:
                separator[part, :] = product

    for copy in edge_halos + rim_halos + [above_halo] + below_halos:
        copy.wait_send()
    for pair in range(len(pairs)):
        for number in range(piece_count):
            bulk(pair, number).wait_send()
    for phase in range(1, phases):
        for slot in range(len(targets[phase])):
            for chunk in range(CHUNKS):
                exchange(phase, slot, chunk).wait_send()


def body(field, right_side, kappa, fronts):
    k_count, depth, width = field.shape
    n_row = lax.axis_size("row")
    n_col = lax.axis_size("col")
    col_bits = n_col.bit_length() - 1
    levels = col_bits + n_row.bit_length() - 1
    groups, targets = phase_plan(levels, col_bits)
    phases = len(targets)
    slots = max(len(target) for target in targets)
    pairs = sum(len(group) == 2 for group in groups)
    f32 = jnp.float32
    dma = pltpu.SemaphoreType.DMA
    regular = pltpu.SemaphoreType.REGULAR
    cube = pltpu.VMEM((k_count, depth, width), f32)
    line = pltpu.VMEM((k_count, width), f32)
    edge = pltpu.VMEM((k_count, LANES), f32)
    rim = pltpu.VMEM((depth, LANES), f32)
    arrays = (field, right_side, kappa, fronts)
    return pl.pallas_call(
        functools.partial(kernel, (k_count, depth, width, levels, col_bits, n_row, n_col)),
        out_shape=(
            jax.ShapeDtypeStruct((k_count, depth, width), f32),
            jax.ShapeDtypeStruct((k_count, width), f32),
        ),
        in_specs=[pl.BlockSpec(memory_space=pl.ANY)] * 4,
        out_specs=(pl.BlockSpec(memory_space=pltpu.VMEM),) * 2,
        scratch_shapes=[
            cube,
            cube,
            pltpu.VMEM((depth, width), f32),
            pltpu.VMEM((levels, width, width), jnp.bfloat16),
            pltpu.VMEM((levels, width, width), jnp.bfloat16),
            pltpu.VMEM((pairs, width, width), jnp.bfloat16),
            pltpu.VMEM((pairs, width, width), f32),
            pltpu.VMEM((pairs, width, width), f32),
            line, line, line, line,
            edge, edge,
            rim, rim, rim, rim,
            pltpu.VMEM((phases, k_count, width), f32),
            pltpu.VMEM((phases, slots, k_count, width), f32),
            line,
            pltpu.VMEM((3, k_count, width), f32),
            pltpu.VMEM((levels, CHUNKS, 2 * k_count // CHUNKS, width), f32),
            pltpu.VMEM((levels, CHUNKS, 2 * k_count // CHUNKS, width), f32),
            pltpu.VMEM((2, k_count, width), f32),
            pltpu.VMEM((HOP_SLOTS, width, width), f32),
            pltpu.VMEM((levels, width, width), f32),
            pltpu.VMEM((levels, width, width), jnp.bfloat16),
            dma((3,)),
            dma((levels,)),
            dma((5 + CHUNKS,)),
            dma((5 + CHUNKS,)),
            dma((phases, slots, 2 * CHUNKS)),
            dma((phases, slots, CHUNKS)),
            dma((pairs, width // PIECE)),
            dma((pairs, width // PIECE)),
            regular((col_bits, 2)),
            regular((levels - col_bits, 2)),
            dma((3, CHUNKS)),
            dma((3, CHUNKS)),
            dma((levels, CHUNKS)),
            dma((levels, CHUNKS)),
            dma((levels, width // LANES)),
            dma((levels, width // LANES)),
        ],
        compiler_params=pltpu.CompilerParams(
            collective_id=0, has_side_effects=True, vmem_limit_bytes=48 << 20
        ),
    )(*(pltpu.with_memory_space_constraint(array, pltpu.HBM) for array in arrays))


def solution(mesh):
    placed = (P(None, "row", "col"), P(None, "row", "col"), P("row", "col"), P(None, "row", "col"))
    return jax.shard_map(
        body,
        mesh=mesh,
        in_specs=placed,
        out_specs=(P(None, "row", "col"), P("row", "col")),
        check_vma=False,
    )
```

```python
import functools

import jax
import jax.numpy as jnp
from jax import lax
from jax.experimental import pallas as pl
from jax.experimental.pallas import tpu as pltpu
from jax.sharding import PartitionSpec as P

MESH = pl.DeviceIdType.MESH
LANES = 128
CHUNKS = 2
HOP_SLOTS = 4
X_STEP = 1
Y_EARLY = 16
PIECE = 32


def back_groups(levels, col_bits):
    groups = []
    level = levels - 1
    while level >= 0:
        row_pair = level == levels - 1 and level - 1 >= col_bits
        col_pair = level % 2 == 1 and level < col_bits and level <= 1
        if row_pair or col_pair:
            groups.append((level, level - 1))
            level -= 2
        else:
            groups.append((level,))
            level -= 1
    return groups


def group_targets(group, top):
    if len(group) == 1:
        return [group]
    a, b = group
    return [(a,), (a, b)] if top else [(a,), (b,), (a, b)]


def phase_plan(levels, col_bits):
    groups = back_groups(levels, col_bits)
    targets = [group_targets(groups[0], True)]
    for group in groups[1:]:
        targets.append(group_targets(group, False))
    return groups, targets


def kernel(
    sizes,
    field, right_side, kappa, fronts,
    residual, mix_here, mix_there, last_turned, last_extra,
    cells, sources, shift, weights, turned, extra, bulk_out, bulk_in,
    first_row, last_row, below, above, edge_left, edge_right,
    rim_first, rim_last, rim_left, rim_right,
    sent, got, level_zero, first_got, pair_sent, pair_got, top_sent, hop_out, hop_in, twin,
    load_sem, front_sem, halo_send, halo_recv, send_sem, recv_sem, bulk_send, bulk_recv,
    col_ready, row_ready, first_send, first_recv, pair_send, pair_recv, hop_send, hop_recv,
):
    k_count, depth, width, levels, col_bits, n_row, n_col = sizes
    row = lax.axis_index("row")
    col = lax.axis_index("col")
    rows_per = k_count // CHUNKS
    groups, targets = phase_plan(levels, col_bits)
    phases = len(targets)
    pairs = [group for group in groups if len(group) == 2]
    row_bits = levels - col_bits
    piece_count = width // PIECE

    def flip(toggled):
        if toggled[0] < col_bits:
            return {"col": jnp.bitwise_xor(col, sum(1 << level for level in toggled))}
        return {"row": jnp.bitwise_xor(row, sum(1 << (level - col_bits) for level in toggled))}

    def sign(level):
        place = col if level < col_bits else row
        bit = level if level < col_bits else level - col_bits
        upper = jnp.bitwise_and(jnp.right_shift(place, bit), 1)
        return 1.0 - 2.0 * upper.astype(jnp.float32)

    def row_at(step):
        return {"row": lax.rem(row + (n_row + step) % n_row, n_row)}

    def col_at(step):
        return {"col": lax.rem(col + (n_col + step) % n_col, n_col)}

    up, down, left, right = row_at(-1), row_at(1), col_at(-1), col_at(1)

    barrier = pltpu.get_barrier_semaphore()
    core = lax.rem(row, 2)
    other_core = {"row": jnp.bitwise_xor(row, 1)}
    across = {"row": jnp.bitwise_xor(row, 1), "col": jnp.bitwise_xor(col, 1)}
    friends = [up, down, left, right, across] + [flip((b,)) for a, b in pairs]
    for friend in friends:
        pl.semaphore_signal(barrier, inc=1, device_id=friend, device_id_type=MESH)

    def tell(step):
        for ready, at, bits in ((col_ready, col_at, col_bits), (row_ready, row_at, row_bits)):
            if step < bits:
                for way, sense in ((0, 1), (1, -1)):
                    pl.semaphore_signal(
                        ready.at[step, way],
                        inc=1,
                        device_id=at(sense * (1 << (step - 1))),
                        device_id_type=MESH,
                    )

    def hear(step):
        for ready, bits in ((col_ready, col_bits), (row_ready, row_bits)):
            if step < bits:
                for way in range(2):
                    pl.semaphore_wait(ready.at[step, way], 1)

    loads = [
        pltpu.make_async_copy(field, cells, load_sem.at[0]),
        pltpu.make_async_copy(right_side, sources, load_sem.at[1]),
        pltpu.make_async_copy(kappa, shift, load_sem.at[2]),
    ]
    front_loads = [
        pltpu.make_async_copy(fronts.at[level], weights.at[level], front_sem.at[level])
        for level in range(levels)
    ]
    loads[0].start()
    front_loads[0].start()
    loads[1].start()
    loads[2].start()
    order = [1, 2] + [a for a, b in pairs if a != 1]
    order += [level for level in range(1, levels) if level not in order]
    for level in order:
        front_loads[level].start()

    def halo(slot, source, target, device):
        return pltpu.make_async_remote_copy(
            src_ref=source,
            dst_ref=target,
            send_sem=halo_send.at[slot],
            recv_sem=halo_recv.at[slot],
            device_id=device,
            device_id_type=MESH,
        )

    def chunk_rows(chunk):
        return pl.ds(chunk * rows_per, rows_per)

    edge_halos = [
        halo(0, last_row.at[:, pl.ds(width - LANES, LANES)], edge_left, right),
        halo(1, last_row.at[:, pl.ds(0, LANES)], edge_right, left),
    ]
    rim_halos = [
        halo(2, rim_last, rim_left, right),
        halo(3, rim_first, rim_right, left),
    ]
    above_halo = halo(4, last_row, above, down)
    below_halos = [
        halo(5 + chunk, first_row.at[chunk_rows(chunk)], below.at[chunk_rows(chunk)], up)
        for chunk in range(CHUNKS)
    ]

    def bulk(pair, piece):
        part = pl.ds(piece * PIECE, PIECE)
        return pltpu.make_async_remote_copy(
            src_ref=bulk_out.at[pair, part],
            dst_ref=bulk_in.at[pair, part],
            send_sem=bulk_send.at[pair, piece],
            recv_sem=bulk_recv.at[pair, piece],
            device_id=flip((pairs[pair][1],)),
            device_id_type=MESH,
        )

    def bulk_start(pair, piece):
        part = pl.ds(piece * PIECE, PIECE)
        level = pairs[pair][0]
        block = last_turned[level, part] if level < 2 else turned[level, part]
        bulk_out[pair, part] = block.astype(jnp.float32)
        bulk(pair, piece).start()

    def bulk_take(pair, piece):
        part = pl.ds(piece * PIECE, PIECE)
        bulk(pair, piece).wait_recv()
        block = bulk_in[pair, part].astype(jnp.bfloat16)
        if pairs[pair][0] < 2:
            last_extra[part, :] = block
        else:
            extra[pair, part] = block

    def turn(level, block):
        part = pl.ds(block * LANES, LANES)
        block = weights[level, :, part].T
        if level < 2:
            last_turned[level, part, :] = block
        else:
            turned[level, part, :] = block

    loads[0].wait()
    first_row[...] = cells[:, 0, :]
    last_row[...] = cells[:, depth - 1, :]
    pl.semaphore_wait(barrier, len(friends))
    for copy in edge_halos + below_halos:
        copy.start()
    tell(1)
    above_halo.start()

    rim_lane = lax.broadcasted_iota(jnp.int32, (depth, LANES), 1)
    firsts = jnp.zeros((depth, LANES), jnp.float32)
    lasts = jnp.zeros((depth, LANES), jnp.float32)
    for k in range(k_count):
        head = cells[k, :, pl.ds(0, LANES)]
        tail = cells[k, :, pl.ds(width - LANES, LANES)]
        firsts = jnp.where(rim_lane == k, pltpu.roll(head, k, 1) if k else head, firsts)
        lasts = jnp.where(rim_lane == k, pltpu.roll(tail, k + 1, 1), lasts)
    rim_first[...] = firsts
    rim_last[...] = lasts
    for copy in rim_halos:
        copy.start()

    has_above = (row > 0).astype(jnp.float32)
    has_below = (row < n_row - 1).astype(jnp.float32)
    has_left = (col > 0).astype(jnp.float32)
    has_right = (col < n_col - 1).astype(jnp.float32)

    def beside(block, right_edge, left_edge):
        lane = lax.broadcasted_iota(jnp.int32, block.shape, 1)
        from_right = jnp.where(lane == width - 1, right_edge, pltpu.roll(block, width - 1, 1))
        from_left = jnp.where(lane == 0, left_edge, pltpu.roll(block, 1, 1))
        return from_right, from_left

    def times(state, front):
        return lax.dot_general(
            state.astype(jnp.bfloat16),
            front,
            (((1,), (0,)), ((), ())),
            preferred_element_type=jnp.float32,
        )

    def exchange(phase, slot, chunk):
        part = chunk_rows(chunk)
        return pltpu.make_async_remote_copy(
            src_ref=sent.at[phase, part],
            dst_ref=got.at[phase, slot, part],
            send_sem=send_sem.at[phase, slot, chunk],
            recv_sem=recv_sem.at[phase, slot, chunk],
            device_id=flip(targets[phase][slot]),
            device_id_type=MESH,
        )

    def send(phase, chunk, value):
        sent[phase, chunk_rows(chunk)] = value
        for slot in range(len(targets[phase])):
            exchange(phase, slot, chunk).start()

    def receive(phase, chunk):
        values = []
        for slot in range(len(targets[phase])):
            exchange(phase, slot, chunk).wait_recv()
            values.append(got[phase, slot, chunk_rows(chunk)])
        return values

    def piece(k):
        block = cells[k]
        line = lax.broadcasted_iota(jnp.int32, block.shape, 0)
        under = jnp.where(
            line == depth - 1, below[pl.ds(k, 1), :] * has_below, pltpu.roll(block, depth - 1, 0)
        )
        over = jnp.where(line == 0, above[pl.ds(k, 1), :] * has_above, pltpu.roll(block, 1, 0))
        from_right, from_left = beside(
            block,
            rim_right[:, pl.ds(k, 1)] * has_right,
            rim_left[:, pl.ds(k, 1)] * has_left,
        )
        near = under + over + from_right + from_left
        residual[k] = sources[k] - ((4.0 + shift[...]) * block - near)

    top_level = levels - 1
    local = col_bits

    def first(slot, chunk):
        part = chunk_rows(chunk)
        return pltpu.make_async_remote_copy(
            src_ref=level_zero.at[part],
            dst_ref=first_got.at[slot, part],
            send_sem=first_send.at[slot, chunk],
            recv_sem=first_recv.at[slot, chunk],
            device_id=(other_core, across, flip((0,)))[slot],
            device_id_type=MESH,
        )

    def pair_copy(level, chunk):
        return pltpu.make_async_remote_copy(
            src_ref=pair_sent.at[level, chunk],
            dst_ref=pair_got.at[level, chunk],
            send_sem=pair_send.at[level, chunk],
            recv_sem=pair_recv.at[level, chunk],
            device_id=flip((level,)),
            device_id_type=MESH,
        )

    def top_copy(owner, slot, chunk):
        part = chunk_rows(chunk)
        steps = sum(1 << (level - col_bits) for level in targets[0][slot])
        return pltpu.make_async_remote_copy(
            src_ref=top_sent.at[owner, part],
            dst_ref=got.at[0, slot, part],
            send_sem=send_sem.at[0, slot, owner * CHUNKS + chunk],
            recv_sem=recv_sem.at[0, slot, chunk],
            device_id={"row": jnp.bitwise_xor(row, steps + 1 - owner)},
            device_id_type=MESH,
        )

    hop_pieces = width // LANES

    def hop(level, piece):
        part = pl.ds(piece * LANES, LANES)
        return pltpu.make_async_remote_copy(
            src_ref=hop_out.at[level % HOP_SLOTS, part],
            dst_ref=hop_in.at[level, part],
            send_sem=hop_send.at[level, piece],
            recv_sem=hop_recv.at[level, piece],
            device_id=other_core,
            device_id_type=MESH,
        )

    def hop_start(level):
        for number in range(hop_pieces):
            part = pl.ds(number * LANES, LANES)
            hop_out[level % HOP_SLOTS, part] = weights[level, part].astype(jnp.float32)
            hop(level, number).start()

    def hop_sent(level):
        for number in range(hop_pieces):
            hop(level, number).wait_send()

    def hop_take(level):
        for number in range(hop_pieces):
            part = pl.ds(number * LANES, LANES)
            hop(level, number).wait_recv()
            twin[level, part] = hop_in[level, part].astype(jnp.bfloat16)

    def spread(tasks, spots):
        out = [[] for _ in range(spots)]
        for index, task in enumerate(tasks):
            out[index * spots // len(tasks)].append(task)
        return out

    starts = []
    takes = []
    for number in range(len(pairs)):
        starts.append([functools.partial(bulk_start, number, p) for p in range(piece_count)])
        takes.append([functools.partial(bulk_take, number, p) for p in range(piece_count)])
    blocks = width // LANES
    ready_turns = [a for a, b in pairs if a != 1]
    early = []
    for number, (a, b) in enumerate(pairs):
        if a != 1:
            early += starts[number][:Y_EARLY]
            starts[number] = starts[number][Y_EARLY:]
    late_turns = [
        [functools.partial(turn, level, block) for block in range(blocks)]
        for level in range(levels)
        if level not in ready_turns and level != 1
    ]
    residual_tasks = [functools.partial(piece, k) for k in range(k_count)]

    front_loads[1].wait()

    @pl.when(core == 0)
    def _():
        hop_start(1)
        front_loads[2].wait()
        hop_start(2)

    for a, b in pairs:
        if a != 1:
            front_loads[a].wait()
            for block in range(blocks):
                turn(a, block)
    for task in early:
        task()

    loads[1].wait()
    loads[2].wait()
    front_loads[0].wait()
    shift_last = shift[pl.ds(depth - 1, 1), :]
    for copy in edge_halos:
        copy.wait_recv()
    for chunk in range(CHUNKS):
        part = chunk_rows(chunk)
        block = last_row[part, :]
        from_right, from_left = beside(
            block,
            edge_right[part, pl.ds(0, 1)] * has_right,
            edge_left[part, pl.ds(LANES - 1, 1)] * has_left,
        )
        below_halos[chunk].wait_recv()
        near = below[part, :] * has_below + cells[part, depth - 2, :] + from_right + from_left
        state = sources[part, depth - 1, :] - ((4.0 + shift_last) * block - near)
        product = times(state, weights[0])
        level_zero[part, :] = product

        @pl.when(core == 0)
        def _():
            first(1, chunk).start()
            first(0, chunk).start()

        @pl.when(core == 1)
        def _():
            first(2, chunk).start()

    @pl.when(core == 1)
    def _():
        front_loads[2].wait()

    for level in range(3, levels):
        if level not in ready_turns:
            front_loads[level].wait()
    above_halo.wait_recv()
    for copy in rim_halos:
        copy.wait_recv()

    @pl.when(core == 0)
    def _():
        for level in range(1, levels):
            hear(level)
            tell(level + 1)
        steps = list(range(3, levels))
        plans = [[] for _ in steps]
        rest = []

        def add(first_step, tasks):
            spots = len(steps) - min(first_step, len(steps) - 1)
            for at, part in enumerate(spread(tasks, spots)):
                plans[len(steps) - spots + at] += part

        for number, (a, b) in enumerate(pairs):
            if a >= col_bits:
                add(0, starts[number])
            else:
                add(0, [functools.partial(turn, 1, block) for block in range(blocks)])
                add(X_STEP, starts[number])
        for at, tasks in enumerate(spread(sum(late_turns, []) + residual_tasks, len(steps))):
            plans[at] += tasks
        for at, level in enumerate(steps):
            if level > HOP_SLOTS:
                hop_sent(level - HOP_SLOTS)
            hop_start(level)
            for task in plans[at]:
                task()
        for task in rest:
            task()
        if pairs[0][0] >= col_bits:
            for task in takes[0]:
                task()
        for level in range(max(1, levels - HOP_SLOTS), levels):
            hop_sent(level)
        for slot in range(2):
            for chunk in range(CHUNKS):
                first(slot, chunk).wait_send()

    @pl.when(core == 1)
    def _():
        stages = [level for level in range(1, levels) if level != local + 1]
        plans = [[] for _ in stages]

        def add(first_level, last_level, tasks):
            spots = [at for at, level in enumerate(stages) if first_level <= level <= last_level]
            spots = spots or [len(stages) - 1]
            for at, part in zip(spots, spread(tasks, len(spots))):
                plans[at] += part

        for number, (a, b) in enumerate(pairs):
            if a >= col_bits:
                add(1, levels - 2, starts[number])
                add(levels - 1, levels - 1, takes[number])
            else:
                add(1, 1, [functools.partial(turn, 1, block) for block in range(blocks)])
                add(2, levels - 1, starts[number])
        for at, tasks in enumerate(late_turns):
            add(2 + at, 2 + at, tasks)
        add(2, levels - 1, residual_tasks[:k_count // 2])

        def fill(tasks, chunk):
            for index, task in enumerate(tasks):
                if index * CHUNKS // len(tasks) == chunk:
                    task()

        hop_take(1)
        for at, level in enumerate(stages):
            hear(level)
            tell(level + 1)
            if level == local:
                hear(level + 1)
                tell(level + 2)
            for chunk in range(CHUNKS):
                part = chunk_rows(chunk)
                sense = sign(level - 1)
                if level == 1:
                    for slot in range(3):
                        first(slot, chunk).wait_recv()
                    low = first_got[1, part] + sense * first_got[0, part]
                    high = first_got[2, part] + sense * level_zero[part, :]
                else:
                    past = level - 1
                    pair_copy(past, chunk).wait_recv()
                    both = pair_got[past, chunk] + sense * pair_sent[past, chunk]
                    low = both[:rows_per]
                    high = both[rows_per:]
                low = times(low, twin[level])
                high = times(high, weights[level])
                out = level
                if level == local:
                    low, high = low + high, low - high
                    out = level + 1
                    low = times(low, twin[out])
                    high = times(high, weights[out])
                if out == top_level:
                    for owner, value in enumerate((low, high)):
                        top_sent[owner, part] = value
                        for slot in range(len(targets[0])):
                            top_copy(owner, slot, chunk).start()
                else:
                    pair_sent[out, chunk, pl.ds(0, rows_per)] = low
                    pair_sent[out, chunk, pl.ds(rows_per, rows_per)] = high
                    pair_copy(out, chunk).start()
                fill(plans[at], chunk)
            if out < top_level:
                hop_take(out + 1)
                if out + 1 == local:
                    hop_take(out + 2)
        for chunk in range(CHUNKS):
            first(2, chunk).wait_send()
            for level in range(1, top_level):
                if level != local:
                    pair_copy(level, chunk).wait_send()
            for owner in range(2):
                for slot in range(len(targets[0])):
                    top_copy(owner, slot, chunk).wait_send()

    work = [[] for _ in range(phases)]
    for number, (a, b) in enumerate(pairs):
        if a < col_bits:
            work[groups.index((a, b))] += takes[number]

    def fill_back(phase, chunk):
        tasks = work[phase]
        for index, task in enumerate(tasks):
            if index * CHUNKS // len(tasks) == chunk:
                task()

        @pl.when(core == 1)
        def _():
            later = residual_tasks[k_count // 2:]
            for index, task in enumerate(later):
                if index * (phases - 1) * CHUNKS // len(later) == (phase - 1) * CHUNKS + chunk:
                    task()

    for number, group in enumerate(groups):
        phase = number
        if len(group) == 2:
            a, b = group
            spare = pairs.index(group)
        for chunk in range(CHUNKS):
            part = chunk_rows(chunk)
            values = receive(phase, chunk)
            mine = sent[phase, part] if number else None
            if len(group) == 1:
                mix = 2.0 * values[0] if number == 0 else mine - sign(group[0]) * values[0]
                product = times(mix, turned[group[0]])
            else:
                if number == 0:
                    here = 2.0 * values[0]
                    there = 2.0 * values[1]
                else:
                    here = mine - sign(a) * values[0]
                    there = values[1] - sign(a) * values[2]
                if phase + 1 == phases:
                    mix_here[part, :] = here.astype(jnp.bfloat16)
                    mix_there[part, :] = there.astype(jnp.bfloat16)
                    continue
                here = times(here, turned[a])
                there = times(there, extra[spare])
                product = times(here - sign(b) * there, turned[b])
            send(phase + 1, chunk, product)
            fill_back(phase + 1, chunk)

    for copy in edge_halos + rim_halos + [above_halo] + below_halos:
        copy.wait_send()
    for pair in range(len(pairs)):
        for number in range(piece_count):
            bulk(pair, number).wait_send()
    for phase in range(1, phases):
        for slot in range(len(targets[phase])):
            for chunk in range(CHUNKS):
                exchange(phase, slot, chunk).wait_send()


def finish(here, there, turned, extra, inner, residual, separator, held, copy_sem):
    copies = [pltpu.make_async_copy(inner, residual, copy_sem.at[0])]
    copies[0].start()

    def times(state, front):
        return lax.dot_general(
            state, front, (((1,), (0,)), ((), ())), preferred_element_type=jnp.float32
        )

    upper = jnp.bitwise_and(lax.axis_index("col"), 1)
    sign = 1.0 - 2.0 * upper.astype(jnp.float32)
    mix = times(here[...], turned[1]) - sign * times(there[...], extra[...])
    held[...] = times(mix.astype(jnp.bfloat16), turned[0])
    copies.append(pltpu.make_async_copy(held, separator, copy_sem.at[1]))
    copies[1].start()
    for copy in copies:
        copy.wait()


def body(field, right_side, kappa, fronts):
    k_count, depth, width = field.shape
    n_row = lax.axis_size("row")
    n_col = lax.axis_size("col")
    col_bits = n_col.bit_length() - 1
    levels = col_bits + n_row.bit_length() - 1
    groups, targets = phase_plan(levels, col_bits)
    phases = len(targets)
    slots = max(len(target) for target in targets)
    pairs = sum(len(group) == 2 for group in groups)
    f32 = jnp.float32
    dma = pltpu.SemaphoreType.DMA
    regular = pltpu.SemaphoreType.REGULAR
    cube = pltpu.VMEM((k_count, depth, width), f32)
    line = pltpu.VMEM((k_count, width), f32)
    edge = pltpu.VMEM((k_count, LANES), f32)
    rim = pltpu.VMEM((depth, LANES), f32)
    arrays = (field, right_side, kappa, fronts)
    residual, *rest = pl.pallas_call(
        functools.partial(kernel, (k_count, depth, width, levels, col_bits, n_row, n_col)),
        out_shape=(
            jax.ShapeDtypeStruct((k_count, depth, width), f32),
            jax.ShapeDtypeStruct((k_count, width), jnp.bfloat16),
            jax.ShapeDtypeStruct((k_count, width), jnp.bfloat16),
            jax.ShapeDtypeStruct((2, width, width), jnp.bfloat16),
            jax.ShapeDtypeStruct((width, width), jnp.bfloat16),
        ),
        in_specs=[pl.BlockSpec(memory_space=pl.ANY)] * 4,
        out_specs=(pl.BlockSpec(memory_space=pltpu.VMEM),) * 5,
        scratch_shapes=[
            cube,
            cube,
            pltpu.VMEM((depth, width), f32),
            pltpu.VMEM((levels, width, width), jnp.bfloat16),
            pltpu.VMEM((levels, width, width), jnp.bfloat16),
            pltpu.VMEM((pairs, width, width), jnp.bfloat16),
            pltpu.VMEM((pairs, width, width), f32),
            pltpu.VMEM((pairs, width, width), f32),
            line, line, line, line,
            edge, edge,
            rim, rim, rim, rim,
            pltpu.VMEM((phases, k_count, width), f32),
            pltpu.VMEM((phases, slots, k_count, width), f32),
            line,
            pltpu.VMEM((3, k_count, width), f32),
            pltpu.VMEM((levels, CHUNKS, 2 * k_count // CHUNKS, width), f32),
            pltpu.VMEM((levels, CHUNKS, 2 * k_count // CHUNKS, width), f32),
            pltpu.VMEM((2, k_count, width), f32),
            pltpu.VMEM((HOP_SLOTS, width, width), f32),
            pltpu.VMEM((levels, width, width), f32),
            pltpu.VMEM((levels, width, width), jnp.bfloat16),
            dma((3,)),
            dma((levels,)),
            dma((5 + CHUNKS,)),
            dma((5 + CHUNKS,)),
            dma((phases, slots, 2 * CHUNKS)),
            dma((phases, slots, CHUNKS)),
            dma((pairs, width // PIECE)),
            dma((pairs, width // PIECE)),
            regular((col_bits, 2)),
            regular((levels - col_bits, 2)),
            dma((3, CHUNKS)),
            dma((3, CHUNKS)),
            dma((levels, CHUNKS)),
            dma((levels, CHUNKS)),
            dma((levels, width // LANES)),
            dma((levels, width // LANES)),
        ],
        compiler_params=pltpu.CompilerParams(
            collective_id=0, has_side_effects=True, vmem_limit_bytes=48 << 20
        ),
    )(*(pltpu.with_memory_space_constraint(array, pltpu.HBM) for array in arrays))
    return pl.pallas_call(
        finish,
        out_shape=(
            jax.ShapeDtypeStruct((k_count, depth, width), f32),
            jax.ShapeDtypeStruct((k_count, width), f32),
        ),
        in_specs=[pl.BlockSpec(memory_space=pltpu.VMEM)] * 5,
        out_specs=(pl.BlockSpec(memory_space=pl.ANY),) * 2,
        scratch_shapes=[line, dma((2,))],
        compiler_params=pltpu.CompilerParams(vmem_limit_bytes=8 << 20),
    )(*rest, residual)


def solution(mesh):
    placed = (P(None, "row", "col"), P(None, "row", "col"), P("row", "col"), P(None, "row", "col"))
    return jax.shard_map(
        body,
        mesh=mesh,
        in_specs=placed,
        out_specs=(P(None, "row", "col"), P("row", "col")),
        check_vma=False,
    )
```

```python
import functools

import jax
import jax.numpy as jnp
from jax import lax
from jax.experimental import pallas as pl
from jax.experimental.pallas import tpu as pltpu
from jax.sharding import PartitionSpec as P

MESH = pl.DeviceIdType.MESH
LANES = 128
CHUNKS = 2
HOP_SLOTS = 4
X_STEP = 1
Y_EARLY = 16
PIECE = 32


def back_groups(levels, col_bits):
    groups = []
    level = levels - 1
    while level >= 0:
        row_pair = level == levels - 1 and level - 1 >= col_bits
        col_pair = level % 2 == 1 and level < col_bits and level <= 1
        if row_pair or col_pair:
            groups.append((level, level - 1))
            level -= 2
        else:
            groups.append((level,))
            level -= 1
    return groups


def group_targets(group, top):
    if len(group) == 1:
        return [group]
    a, b = group
    return [(a,), (a, b)] if top else [(a,), (b,), (a, b)]


def phase_plan(levels, col_bits):
    groups = back_groups(levels, col_bits)
    targets = [group_targets(groups[0], True)]
    for group in groups[1:]:
        targets.append(group_targets(group, False))
    return groups, targets


def kernel(
    sizes,
    field, right_side, kappa, fronts,
    residual, mix_here, mix_there, last_turned, last_extra,
    cells, sources, shift, weights, turned, extra, bulk_out, bulk_in,
    first_row, last_row, below, above, edge_left, edge_right,
    rim_first, rim_last, rim_left, rim_right,
    sent, got, level_zero, first_got, pair_sent, pair_got, top_sent, hop_out, hop_in, twin,
    load_sem, front_sem, halo_send, halo_recv, send_sem, recv_sem, bulk_send, bulk_recv,
    col_ready, row_ready, first_send, first_recv, pair_send, pair_recv, hop_send, hop_recv,
):
    k_count, depth, width, levels, col_bits, n_row, n_col = sizes
    row = lax.axis_index("row")
    col = lax.axis_index("col")
    rows_per = k_count // CHUNKS
    groups, targets = phase_plan(levels, col_bits)
    phases = len(targets)
    pairs = [group for group in groups if len(group) == 2]
    row_bits = levels - col_bits
    piece_count = width // PIECE

    def flip(toggled):
        if toggled[0] < col_bits:
            return {"col": jnp.bitwise_xor(col, sum(1 << level for level in toggled))}
        return {"row": jnp.bitwise_xor(row, sum(1 << (level - col_bits) for level in toggled))}

    def sign(level):
        place = col if level < col_bits else row
        bit = level if level < col_bits else level - col_bits
        upper = jnp.bitwise_and(jnp.right_shift(place, bit), 1)
        return 1.0 - 2.0 * upper.astype(jnp.float32)

    def row_at(step):
        return {"row": lax.rem(row + (n_row + step) % n_row, n_row)}

    def col_at(step):
        return {"col": lax.rem(col + (n_col + step) % n_col, n_col)}

    up, down, left, right = row_at(-1), row_at(1), col_at(-1), col_at(1)

    barrier = pltpu.get_barrier_semaphore()
    core = lax.rem(row, 2)
    other_core = {"row": jnp.bitwise_xor(row, 1)}
    across = {"row": jnp.bitwise_xor(row, 1), "col": jnp.bitwise_xor(col, 1)}
    friends = [up, down, left, right, across] + [flip((b,)) for a, b in pairs]
    for friend in friends:
        pl.semaphore_signal(barrier, inc=1, device_id=friend, device_id_type=MESH)

    def tell(step):
        for ready, at, bits in ((col_ready, col_at, col_bits), (row_ready, row_at, row_bits)):
            if step < bits:
                for way, sense in ((0, 1), (1, -1)):
                    pl.semaphore_signal(
                        ready.at[step, way],
                        inc=1,
                        device_id=at(sense * (1 << (step - 1))),
                        device_id_type=MESH,
                    )

    def hear(step):
        for ready, bits in ((col_ready, col_bits), (row_ready, row_bits)):
            if step < bits:
                for way in range(2):
                    pl.semaphore_wait(ready.at[step, way], 1)

    loads = [
        pltpu.make_async_copy(field, cells, load_sem.at[0]),
        pltpu.make_async_copy(right_side, sources, load_sem.at[1]),
        pltpu.make_async_copy(kappa, shift, load_sem.at[2]),
    ]
    front_loads = [
        pltpu.make_async_copy(fronts.at[level], weights.at[level], front_sem.at[level])
        for level in range(levels)
    ]
    loads[0].start()

    def halo(slot, source, target, device):
        return pltpu.make_async_remote_copy(
            src_ref=source,
            dst_ref=target,
            send_sem=halo_send.at[slot],
            recv_sem=halo_recv.at[slot],
            device_id=device,
            device_id_type=MESH,
        )

    def chunk_rows(chunk):
        return pl.ds(chunk * rows_per, rows_per)

    edge_halos = [
        halo(0, last_row.at[:, pl.ds(width - LANES, LANES)], edge_left, right),
        halo(1, last_row.at[:, pl.ds(0, LANES)], edge_right, left),
    ]
    rim_halos = [
        halo(2, rim_last, rim_left, right),
        halo(3, rim_first, rim_right, left),
    ]
    above_halo = halo(4, last_row, above, down)
    below_halos = [
        halo(5 + chunk, first_row.at[chunk_rows(chunk)], below.at[chunk_rows(chunk)], up)
        for chunk in range(CHUNKS)
    ]

    def bulk(pair, piece):
        part = pl.ds(piece * PIECE, PIECE)
        return pltpu.make_async_remote_copy(
            src_ref=bulk_out.at[pair, part],
            dst_ref=bulk_in.at[pair, part],
            send_sem=bulk_send.at[pair, piece],
            recv_sem=bulk_recv.at[pair, piece],
            device_id=flip((pairs[pair][1],)),
            device_id_type=MESH,
        )

    def bulk_start(pair, piece):
        part = pl.ds(piece * PIECE, PIECE)
        level = pairs[pair][0]
        block = last_turned[level, part] if level < 2 else turned[level, part]
        bulk_out[pair, part] = block.astype(jnp.float32)
        bulk(pair, piece).start()

    def bulk_take(pair, piece):
        part = pl.ds(piece * PIECE, PIECE)
        bulk(pair, piece).wait_recv()
        block = bulk_in[pair, part].astype(jnp.bfloat16)
        if pairs[pair][0] < 2:
            last_extra[part, :] = block
        else:
            extra[pair, part] = block

    def turn(level, block):
        part = pl.ds(block * LANES, LANES)
        block = weights[level, :, part].T
        if level < 2:
            last_turned[level, part, :] = block
        else:
            turned[level, part, :] = block

    loads[0].wait()
    front_loads[0].start()
    loads[1].start()
    loads[2].start()
    order = [1, 2] + [a for a, b in pairs if a != 1]
    order += [level for level in range(1, levels) if level not in order]
    for level in order:
        front_loads[level].start()
    first_row[...] = cells[:, 0, :]
    last_row[...] = cells[:, depth - 1, :]
    pl.semaphore_wait(barrier, len(friends))
    for copy in edge_halos + below_halos:
        copy.start()
    tell(1)
    above_halo.start()

    rim_lane = lax.broadcasted_iota(jnp.int32, (depth, LANES), 1)
    firsts = jnp.zeros((depth, LANES), jnp.float32)
    lasts = jnp.zeros((depth, LANES), jnp.float32)
    for k in range(k_count):
        head = cells[k, :, pl.ds(0, LANES)]
        tail = cells[k, :, pl.ds(width - LANES, LANES)]
        firsts = jnp.where(rim_lane == k, pltpu.roll(head, k, 1) if k else head, firsts)
        lasts = jnp.where(rim_lane == k, pltpu.roll(tail, k + 1, 1), lasts)
    rim_first[...] = firsts
    rim_last[...] = lasts
    for copy in rim_halos:
        copy.start()

    has_above = (row > 0).astype(jnp.float32)
    has_below = (row < n_row - 1).astype(jnp.float32)
    has_left = (col > 0).astype(jnp.float32)
    has_right = (col < n_col - 1).astype(jnp.float32)

    def beside(block, right_edge, left_edge):
        lane = lax.broadcasted_iota(jnp.int32, block.shape, 1)
        from_right = jnp.where(lane == width - 1, right_edge, pltpu.roll(block, width - 1, 1))
        from_left = jnp.where(lane == 0, left_edge, pltpu.roll(block, 1, 1))
        return from_right, from_left

    def times(state, front):
        return lax.dot_general(
            state.astype(jnp.bfloat16),
            front,
            (((1,), (0,)), ((), ())),
            preferred_element_type=jnp.float32,
        )

    def exchange(phase, slot, chunk):
        part = chunk_rows(chunk)
        return pltpu.make_async_remote_copy(
            src_ref=sent.at[phase, part],
            dst_ref=got.at[phase, slot, part],
            send_sem=send_sem.at[phase, slot, chunk],
            recv_sem=recv_sem.at[phase, slot, chunk],
            device_id=flip(targets[phase][slot]),
            device_id_type=MESH,
        )

    def send(phase, chunk, value):
        sent[phase, chunk_rows(chunk)] = value
        for slot in range(len(targets[phase])):
            exchange(phase, slot, chunk).start()

    def receive(phase, chunk):
        values = []
        for slot in range(len(targets[phase])):
            exchange(phase, slot, chunk).wait_recv()
            values.append(got[phase, slot, chunk_rows(chunk)])
        return values

    def piece(k):
        block = cells[k]
        line = lax.broadcasted_iota(jnp.int32, block.shape, 0)
        under = jnp.where(
            line == depth - 1, below[pl.ds(k, 1), :] * has_below, pltpu.roll(block, depth - 1, 0)
        )
        over = jnp.where(line == 0, above[pl.ds(k, 1), :] * has_above, pltpu.roll(block, 1, 0))
        from_right, from_left = beside(
            block,
            rim_right[:, pl.ds(k, 1)] * has_right,
            rim_left[:, pl.ds(k, 1)] * has_left,
        )
        near = under + over + from_right + from_left
        residual[k] = sources[k] - ((4.0 + shift[...]) * block - near)

    top_level = levels - 1
    local = col_bits

    def first(slot, chunk):
        part = chunk_rows(chunk)
        return pltpu.make_async_remote_copy(
            src_ref=level_zero.at[part],
            dst_ref=first_got.at[slot, part],
            send_sem=first_send.at[slot, chunk],
            recv_sem=first_recv.at[slot, chunk],
            device_id=(other_core, across, flip((0,)))[slot],
            device_id_type=MESH,
        )

    def pair_copy(level, chunk):
        return pltpu.make_async_remote_copy(
            src_ref=pair_sent.at[level, chunk],
            dst_ref=pair_got.at[level, chunk],
            send_sem=pair_send.at[level, chunk],
            recv_sem=pair_recv.at[level, chunk],
            device_id=flip((level,)),
            device_id_type=MESH,
        )

    def top_copy(owner, slot, chunk):
        part = chunk_rows(chunk)
        steps = sum(1 << (level - col_bits) for level in targets[0][slot])
        return pltpu.make_async_remote_copy(
            src_ref=top_sent.at[owner, part],
            dst_ref=got.at[0, slot, part],
            send_sem=send_sem.at[0, slot, owner * CHUNKS + chunk],
            recv_sem=recv_sem.at[0, slot, chunk],
            device_id={"row": jnp.bitwise_xor(row, steps + 1 - owner)},
            device_id_type=MESH,
        )

    hop_pieces = width // LANES

    def hop(level, piece):
        part = pl.ds(piece * LANES, LANES)
        return pltpu.make_async_remote_copy(
            src_ref=hop_out.at[level % HOP_SLOTS, part],
            dst_ref=hop_in.at[level, part],
            send_sem=hop_send.at[level, piece],
            recv_sem=hop_recv.at[level, piece],
            device_id=other_core,
            device_id_type=MESH,
        )

    def hop_start(level):
        for number in range(hop_pieces):
            part = pl.ds(number * LANES, LANES)
            hop_out[level % HOP_SLOTS, part] = weights[level, part].astype(jnp.float32)
            hop(level, number).start()

    def hop_sent(level):
        for number in range(hop_pieces):
            hop(level, number).wait_send()

    def hop_take(level):
        for number in range(hop_pieces):
            part = pl.ds(number * LANES, LANES)
            hop(level, number).wait_recv()
            twin[level, part] = hop_in[level, part].astype(jnp.bfloat16)

    def spread(tasks, spots):
        out = [[] for _ in range(spots)]
        for index, task in enumerate(tasks):
            out[index * spots // len(tasks)].append(task)
        return out

    starts = []
    takes = []
    for number in range(len(pairs)):
        starts.append([functools.partial(bulk_start, number, p) for p in range(piece_count)])
        takes.append([functools.partial(bulk_take, number, p) for p in range(piece_count)])
    blocks = width // LANES
    ready_turns = [a for a, b in pairs if a != 1]
    early = []
    for number, (a, b) in enumerate(pairs):
        if a != 1:
            early += starts[number][:Y_EARLY]
            starts[number] = starts[number][Y_EARLY:]
    late_turns = [
        [functools.partial(turn, level, block) for block in range(blocks)]
        for level in range(levels)
        if level not in ready_turns and level != 1
    ]
    residual_tasks = [functools.partial(piece, k) for k in range(k_count)]

    front_loads[1].wait()

    @pl.when(core == 0)
    def _():
        hop_start(1)
        front_loads[2].wait()
        hop_start(2)

    for a, b in pairs:
        if a != 1:
            front_loads[a].wait()
            for block in range(blocks):
                turn(a, block)
    for task in early:
        task()

    loads[1].wait()
    loads[2].wait()
    front_loads[0].wait()
    shift_last = shift[pl.ds(depth - 1, 1), :]
    for copy in edge_halos:
        copy.wait_recv()
    for chunk in range(CHUNKS):
        part = chunk_rows(chunk)
        block = last_row[part, :]
        from_right, from_left = beside(
            block,
            edge_right[part, pl.ds(0, 1)] * has_right,
            edge_left[part, pl.ds(LANES - 1, 1)] * has_left,
        )
        below_halos[chunk].wait_recv()
        near = below[part, :] * has_below + cells[part, depth - 2, :] + from_right + from_left
        state = sources[part, depth - 1, :] - ((4.0 + shift_last) * block - near)
        product = times(state, weights[0])
        level_zero[part, :] = product

        @pl.when(core == 0)
        def _():
            first(1, chunk).start()
            first(0, chunk).start()

        @pl.when(core == 1)
        def _():
            first(2, chunk).start()

    @pl.when(core == 1)
    def _():
        front_loads[2].wait()

    for level in range(3, levels):
        if level not in ready_turns:
            front_loads[level].wait()
    above_halo.wait_recv()
    for copy in rim_halos:
        copy.wait_recv()

    @pl.when(core == 0)
    def _():
        for level in range(1, levels):
            hear(level)
            tell(level + 1)
        steps = list(range(3, levels))
        plans = [[] for _ in steps]
        rest = []

        def add(first_step, tasks):
            spots = len(steps) - min(first_step, len(steps) - 1)
            for at, part in enumerate(spread(tasks, spots)):
                plans[len(steps) - spots + at] += part

        for number, (a, b) in enumerate(pairs):
            if a >= col_bits:
                add(0, starts[number])
            else:
                add(0, [functools.partial(turn, 1, block) for block in range(blocks)])
                add(X_STEP, starts[number])
        for at, tasks in enumerate(spread(sum(late_turns, []) + residual_tasks, len(steps))):
            plans[at] += tasks
        for at, level in enumerate(steps):
            if level > HOP_SLOTS:
                hop_sent(level - HOP_SLOTS)
            hop_start(level)
            for task in plans[at]:
                task()
        for task in rest:
            task()
        if pairs[0][0] >= col_bits:
            for task in takes[0]:
                task()
        for level in range(max(1, levels - HOP_SLOTS), levels):
            hop_sent(level)
        for slot in range(2):
            for chunk in range(CHUNKS):
                first(slot, chunk).wait_send()

    @pl.when(core == 1)
    def _():
        stages = [level for level in range(1, levels) if level != local + 1]
        plans = [[] for _ in stages]

        def add(first_level, last_level, tasks):
            spots = [at for at, level in enumerate(stages) if first_level <= level <= last_level]
            spots = spots or [len(stages) - 1]
            for at, part in zip(spots, spread(tasks, len(spots))):
                plans[at] += part

        for number, (a, b) in enumerate(pairs):
            if a >= col_bits:
                add(1, levels - 2, starts[number])
                add(levels - 1, levels - 1, takes[number])
            else:
                add(1, 1, [functools.partial(turn, 1, block) for block in range(blocks)])
                add(2, levels - 1, starts[number])
        for at, tasks in enumerate(late_turns):
            add(2 + at, 2 + at, tasks)
        add(2, levels - 1, residual_tasks[:k_count // 2])

        def fill(tasks, chunk):
            for index, task in enumerate(tasks):
                if index * CHUNKS // len(tasks) == chunk:
                    task()

        hop_take(1)
        for at, level in enumerate(stages):
            hear(level)
            tell(level + 1)
            if level == local:
                hear(level + 1)
                tell(level + 2)
            for chunk in range(CHUNKS):
                part = chunk_rows(chunk)
                sense = sign(level - 1)
                if level == 1:
                    for slot in range(3):
                        first(slot, chunk).wait_recv()
                    low = first_got[1, part] + sense * first_got[0, part]
                    high = first_got[2, part] + sense * level_zero[part, :]
                else:
                    past = level - 1
                    pair_copy(past, chunk).wait_recv()
                    both = pair_got[past, chunk] + sense * pair_sent[past, chunk]
                    low = both[:rows_per]
                    high = both[rows_per:]
                low = times(low, twin[level])
                high = times(high, weights[level])
                out = level
                if level == local:
                    low, high = low + high, low - high
                    out = level + 1
                    low = times(low, twin[out])
                    high = times(high, weights[out])
                if out == top_level:
                    for owner, value in enumerate((low, high)):
                        top_sent[owner, part] = value
                        for slot in range(len(targets[0])):
                            top_copy(owner, slot, chunk).start()
                else:
                    pair_sent[out, chunk, pl.ds(0, rows_per)] = low
                    pair_sent[out, chunk, pl.ds(rows_per, rows_per)] = high
                    pair_copy(out, chunk).start()
                fill(plans[at], chunk)
            if out < top_level:
                hop_take(out + 1)
                if out + 1 == local:
                    hop_take(out + 2)
        for chunk in range(CHUNKS):
            first(2, chunk).wait_send()
            for level in range(1, top_level):
                if level != local:
                    pair_copy(level, chunk).wait_send()
            for owner in range(2):
                for slot in range(len(targets[0])):
                    top_copy(owner, slot, chunk).wait_send()

    work = [[] for _ in range(phases)]
    for number, (a, b) in enumerate(pairs):
        if a < col_bits:
            work[groups.index((a, b))] += takes[number]

    def fill_back(phase, chunk):
        tasks = work[phase]
        for index, task in enumerate(tasks):
            if index * CHUNKS // len(tasks) == chunk:
                task()

        @pl.when(core == 1)
        def _():
            later = residual_tasks[k_count // 2:]
            for index, task in enumerate(later):
                if index * (phases - 1) * CHUNKS // len(later) == (phase - 1) * CHUNKS + chunk:
                    task()

    for number, group in enumerate(groups):
        phase = number
        if len(group) == 2:
            a, b = group
            spare = pairs.index(group)
        for chunk in range(CHUNKS):
            part = chunk_rows(chunk)
            values = receive(phase, chunk)
            mine = sent[phase, part] if number else None
            if len(group) == 1:
                mix = 2.0 * values[0] if number == 0 else mine - sign(group[0]) * values[0]
                product = times(mix, turned[group[0]])
            else:
                if number == 0:
                    here = 2.0 * values[0]
                    there = 2.0 * values[1]
                else:
                    here = mine - sign(a) * values[0]
                    there = values[1] - sign(a) * values[2]
                if phase + 1 == phases:
                    mix_here[part, :] = here.astype(jnp.bfloat16)
                    mix_there[part, :] = there.astype(jnp.bfloat16)
                    continue
                here = times(here, turned[a])
                there = times(there, extra[spare])
                product = times(here - sign(b) * there, turned[b])
            send(phase + 1, chunk, product)
            fill_back(phase + 1, chunk)

    for copy in edge_halos + rim_halos + [above_halo] + below_halos:
        copy.wait_send()
    for pair in range(len(pairs)):
        for number in range(piece_count):
            bulk(pair, number).wait_send()
    for phase in range(1, phases):
        for slot in range(len(targets[phase])):
            for chunk in range(CHUNKS):
                exchange(phase, slot, chunk).wait_send()


def finish(here, there, turned, extra, inner, residual, separator, held, copy_sem):
    quarter = inner.shape[0] // 4
    copies = []
    for slot in range(4):
        part = pl.ds(slot * quarter, quarter)
        copies.append(
            pltpu.make_async_copy(inner.at[part], residual.at[part], copy_sem.at[slot])
        )
        copies[slot].start()

    def times(state, front):
        return lax.dot_general(
            state, front, (((1,), (0,)), ((), ())), preferred_element_type=jnp.float32
        )

    upper = jnp.bitwise_and(lax.axis_index("col"), 1)
    sign = 1.0 - 2.0 * upper.astype(jnp.float32)
    mix = times(here[...], turned[1]) - sign * times(there[...], extra[...])
    held[...] = times(mix.astype(jnp.bfloat16), turned[0])
    copies.append(pltpu.make_async_copy(held, separator, copy_sem.at[4]))
    copies[4].start()
    for copy in copies:
        copy.wait()


def body(field, right_side, kappa, fronts):
    k_count, depth, width = field.shape
    n_row = lax.axis_size("row")
    n_col = lax.axis_size("col")
    col_bits = n_col.bit_length() - 1
    levels = col_bits + n_row.bit_length() - 1
    groups, targets = phase_plan(levels, col_bits)
    phases = len(targets)
    slots = max(len(target) for target in targets)
    pairs = sum(len(group) == 2 for group in groups)
    f32 = jnp.float32
    dma = pltpu.SemaphoreType.DMA
    regular = pltpu.SemaphoreType.REGULAR
    cube = pltpu.VMEM((k_count, depth, width), f32)
    line = pltpu.VMEM((k_count, width), f32)
    edge = pltpu.VMEM((k_count, LANES), f32)
    rim = pltpu.VMEM((depth, LANES), f32)
    arrays = (field, right_side, kappa, fronts)
    residual, *rest = pl.pallas_call(
        functools.partial(kernel, (k_count, depth, width, levels, col_bits, n_row, n_col)),
        out_shape=(
            jax.ShapeDtypeStruct((k_count, depth, width), f32),
            jax.ShapeDtypeStruct((k_count, width), jnp.bfloat16),
            jax.ShapeDtypeStruct((k_count, width), jnp.bfloat16),
            jax.ShapeDtypeStruct((2, width, width), jnp.bfloat16),
            jax.ShapeDtypeStruct((width, width), jnp.bfloat16),
        ),
        in_specs=[pl.BlockSpec(memory_space=pl.ANY)] * 4,
        out_specs=(pl.BlockSpec(memory_space=pltpu.VMEM),) * 5,
        scratch_shapes=[
            cube,
            cube,
            pltpu.VMEM((depth, width), f32),
            pltpu.VMEM((levels, width, width), jnp.bfloat16),
            pltpu.VMEM((levels, width, width), jnp.bfloat16),
            pltpu.VMEM((pairs, width, width), jnp.bfloat16),
            pltpu.VMEM((pairs, width, width), f32),
            pltpu.VMEM((pairs, width, width), f32),
            line, line, line, line,
            edge, edge,
            rim, rim, rim, rim,
            pltpu.VMEM((phases, k_count, width), f32),
            pltpu.VMEM((phases, slots, k_count, width), f32),
            line,
            pltpu.VMEM((3, k_count, width), f32),
            pltpu.VMEM((levels, CHUNKS, 2 * k_count // CHUNKS, width), f32),
            pltpu.VMEM((levels, CHUNKS, 2 * k_count // CHUNKS, width), f32),
            pltpu.VMEM((2, k_count, width), f32),
            pltpu.VMEM((HOP_SLOTS, width, width), f32),
            pltpu.VMEM((levels, width, width), f32),
            pltpu.VMEM((levels, width, width), jnp.bfloat16),
            dma((3,)),
            dma((levels,)),
            dma((5 + CHUNKS,)),
            dma((5 + CHUNKS,)),
            dma((phases, slots, 2 * CHUNKS)),
            dma((phases, slots, CHUNKS)),
            dma((pairs, width // PIECE)),
            dma((pairs, width // PIECE)),
            regular((col_bits, 2)),
            regular((levels - col_bits, 2)),
            dma((3, CHUNKS)),
            dma((3, CHUNKS)),
            dma((levels, CHUNKS)),
            dma((levels, CHUNKS)),
            dma((levels, width // LANES)),
            dma((levels, width // LANES)),
        ],
        compiler_params=pltpu.CompilerParams(
            collective_id=0, has_side_effects=True, vmem_limit_bytes=48 << 20
        ),
    )(*(pltpu.with_memory_space_constraint(array, pltpu.HBM) for array in arrays))
    return pl.pallas_call(
        finish,
        out_shape=(
            jax.ShapeDtypeStruct((k_count, depth, width), f32),
            jax.ShapeDtypeStruct((k_count, width), f32),
        ),
        in_specs=[pl.BlockSpec(memory_space=pltpu.VMEM)] * 5,
        out_specs=(pl.BlockSpec(memory_space=pl.ANY),) * 2,
        scratch_shapes=[line, dma((5,))],
        compiler_params=pltpu.CompilerParams(vmem_limit_bytes=8 << 20),
    )(*rest, residual)


def solution(mesh):
    placed = (P(None, "row", "col"), P(None, "row", "col"), P("row", "col"), P(None, "row", "col"))
    return jax.shard_map(
        body,
        mesh=mesh,
        in_specs=placed,
        out_specs=(P(None, "row", "col"), P("row", "col")),
        check_vma=False,
    )
```
